32 devices in a mesh: arcs: 2 (over y), seg: 16 (over z, x, core).
Axes of the slice: x: 2, y: 2, z: 4, core: 2. Of those that a mesh axis runs over, the one named last changes fastest.
Arguments:
- pulses: bfloat16 [2, 8192, 256], P(None, ('arcs', 'seg')), parts along dimension 1, may hold values from -6 to 6
- fraction: float32 [8192], P(('arcs', 'seg')), parts along dimension 0, may hold values from 0 to 1
- gate_shift: int32 [8192], P(('arcs', 'seg')), parts along dimension 0, may hold values from 0 to 15
- aperture_start: int32 [4096], P(('arcs', 'seg')), parts along dimension 0, may hold values from 0 to 4095, as said below
- aperture_end: int32 [4096], P(('arcs', 'seg')), parts along dimension 0, may hold values from 257 to 4096, as said below
- doppler: float32 [4096], P(('arcs', 'seg')), parts along dimension 0, may hold values from -2000 to 2000
- chirp_rate: float32 [4096], P(('arcs', 'seg')), parts along dimension 0, may hold values from 2000 to 6000
Outputs:
- focused: bfloat16 [2, 4096, 256], P(None, ('arcs', 'seg')), parts along dimension 1
- multilook: float32 [4096, 256], P(('arcs', 'seg')), parts along dimension 0
The draws below stay inside these ranges and needn't reach their ends.
There are 2 independent parts, one for each index of `arcs`. The reference program is written for one: setup_inputs(seed, part) draws one part's arguments, and reference() takes and returns one part's arrays. A program takes and returns all parts, laid end to end along the dimension named above; each array names one. Nothing has to cross between parts.
Inputs may be any that keep to these rules, and one draw needn't show every extreme that they name: aperture_start[w] >= (w // 128 - 4) * 256, with equality for some waveform; aperture_end[w] - aperture_start[w] >= 257. aperture_end[w] <= (w // 128 + 5) * 256, with equality for some waveform; aperture_start[w] < aperture_end[w].
All inputs are finite; a program needn't handle non-finite values.
Results may differ from the reference program's by a relative error of at most 0.0064.
Values may be sent and summed in bfloat16 or wider, within the bound.
No kernel may reach another device: no remote copies, remote signals or barrier semaphores. Data moves between devices by JAX's collectives and lax.ppermute only.
A program may use at most 64 MiB of HBM per device.

```python
import jax
import jax.numpy as jnp
from jax import lax

G = 256
P_DEV = 256
W_DEV = 128
REACH = 4
LOOK = 8
SHIFT_MAX = 16
PULSES = 4096
WAVES = 2048
N_SEG = 16


def aperture_pair(key):
    aperture_key = jax.random.fold_in(key, 7321)
    wave_index = jnp.arange(WAVES, dtype=jnp.int32)
    device = wave_index // W_DEV
    within = wave_index % W_DEV
    center = device * P_DEV + within * P_DEV // W_DEV + P_DEV // (2 * W_DEV)
    half_span = jax.random.randint(aperture_key, (WAVES,), P_DEV, REACH * P_DEV + 1, dtype=jnp.int32)
    first_mark = WAVES // 2
    second_mark = WAVES // 2 + W_DEV - 1
    half_span = jnp.where(wave_index == first_mark, REACH * P_DEV + P_DEV // (2 * W_DEV), half_span)
    reach_end = (device + REACH + 1) * P_DEV - 1 - center
    half_span = jnp.where(wave_index == second_mark, reach_end, half_span)
    first_pulse = jnp.maximum(center - half_span, 0)
    last_pulse = jnp.minimum(center + half_span + 1, PULSES)
    return (first_pulse.astype(jnp.int32), last_pulse.astype(jnp.int32))


def draw_aperture_start(key, part):
    return aperture_pair(key)[0]


def draw_aperture_end(key, part):
    return aperture_pair(key)[1]


def with_ends(drawn, rng, smallest, high):
    longest = drawn.shape.index(max(drawn.shape))
    spots = []
    for shift in (0, 1):
        where = [jax.random.randint(jax.random.fold_in(rng, axis), (), 0, length) for axis, length in enumerate(drawn.shape)]
        where[longest] = (where[longest] + shift) % drawn.shape[longest]
        spots.append(tuple(where))
    return drawn.at[spots[0]].set(smallest).at[spots[1]].set(high)


def levels(key, shape, pieces, low, largest):
    gain = 1.0
    for axis_at, parts in pieces:
        draws = jax.random.uniform(jax.random.fold_in(jax.random.fold_in(key, 6), axis_at), (parts,), jnp.float32, low / len(pieces), largest / len(pieces))
        gain = gain * jnp.repeat(jnp.exp(draws), shape[axis_at] // parts).reshape((-1,) + (1,) * (len(shape) - 1 - axis_at))
    return gain


def gaussian(rng, shape, spread, reach, cuts=(), held_as=jnp.bfloat16):
    gain = levels(rng, shape, cuts, -0.22, 0.18) if cuts else 1.0
    values = jax.random.normal(rng, shape, jnp.float32) * spread * gain
    return jnp.minimum(jnp.maximum(values, -reach), reach).astype(held_as)


def setup_inputs(seed: int = 0, part: int = 0) -> dict:
    keys = jax.random.split(jax.random.key(seed), 8)
    part_splits = jax.random.split(jax.random.fold_in(keys[7], part), 8)
    return {
        "pulses": gaussian(part_splits[0], (2, PULSES, G), 1.0, 6.0, ((1, 16),)),
        "fraction": jnp.clip(1.0 * jax.random.uniform(part_splits[1], (PULSES,), jnp.float32) ** levels(part_splits[1], (PULSES,), ((0, 16),), -0.2, 0.2), 0.0, 1.0),
        "gate_shift": with_ends(jax.random.randint(part_splits[2], (PULSES,), 0, SHIFT_MAX), jax.random.fold_in(part_splits[2], 1), 0, SHIFT_MAX - 1).astype(jnp.int32),
        "aperture_start": draw_aperture_start(jax.random.fold_in(jax.random.fold_in(keys[7], part), 71), part),
        "aperture_end": draw_aperture_end(jax.random.fold_in(jax.random.fold_in(keys[7], part), 71), part),
        "doppler": jnp.clip(jax.random.uniform(part_splits[5], (WAVES,), jnp.float32, -2000.0, 2000.0) * levels(part_splits[5], (WAVES,), ((0, 16),), -0.4, 0.0), -2000.0, 2000.0),
        "chirp_rate": jnp.clip(2000.0 + 4000.0 * jax.random.uniform(part_splits[6], (WAVES,), jnp.float32) ** levels(part_splits[6], (WAVES,), ((0, 16),), -0.2, 0.2), 2000.0, 6000.0),
    }


def migrate(pulses, fraction, gate_shift):
    widened = jnp.pad(pulses.astype(jnp.float32), ((0, 0), (0, 0), (0, SHIFT_MAX + 1)))
    blend = fraction[None, :, None]
    shift_col = gate_shift[None, :, None]
    result = jnp.zeros(pulses.shape, jnp.float32)
    for gate_step in range(SHIFT_MAX + 1):
        coeff = jnp.where(shift_col == gate_step, 1.0 - blend, 0.0) + jnp.where(shift_col + 1 == gate_step, blend, 0.0)
        result = result + coeff * widened[:, :, gate_step:gate_step + G]
    return result.astype(jnp.bfloat16)

def weights(first_pulse, last_pulse, doppler, chirp_rate, pulse_index):
    center = (first_pulse + last_pulse) // 2
    relative = (pulse_index[None, :] - center[:, None]).astype(jnp.float32) / float(REACH * P_DEV)
    phase_angle = chirp_rate[:, None] * relative * relative + doppler[:, None] * relative
    inside = (pulse_index[None, :] >= first_pulse[:, None]) & (pulse_index[None, :] < last_pulse[:, None])
    amplitude = lax.rsqrt((last_pulse - first_pulse).astype(jnp.float32))[:, None]
    weight_re = jnp.where(inside, amplitude * jnp.cos(phase_angle), 0.0).astype(jnp.bfloat16)
    weight_im = jnp.where(inside, amplitude * jnp.sin(phase_angle), 0.0).astype(jnp.bfloat16)
    return (weight_re, weight_im)

def focus_block(weight_re, weight_im, block_data):
    real_part = jnp.dot(weight_re, block_data[0], preferred_element_type=jnp.float32) - jnp.dot(weight_im, block_data[1], preferred_element_type=jnp.float32)
    imag_part = jnp.dot(weight_re, block_data[1], preferred_element_type=jnp.float32) + jnp.dot(weight_im, block_data[0], preferred_element_type=jnp.float32)
    return jnp.stack([real_part, imag_part])

def settle(term):
    rounded = lax.optimization_barrier(term.astype(jnp.bfloat16))
    return rounded.astype(jnp.float32)

def reference(pulses, fraction, gate_shift, aperture_start, aperture_end, doppler, chirp_rate):
    migrated = migrate(pulses, fraction, gate_shift)
    padded = jnp.pad(migrated, ((0, 0), (REACH * P_DEV, REACH * P_DEV), (0, 0)))
    window_len = (2 * REACH + 1) * P_DEV

    def one_block(block_index):
        window = lax.dynamic_slice_in_dim(padded, block_index * P_DEV, window_len, 1)
        pulse_index = (block_index - REACH) * P_DEV + jnp.arange(window_len, dtype=jnp.int32)
        first_pulse = lax.dynamic_slice_in_dim(aperture_start, block_index * W_DEV, W_DEV)
        last_pulse = lax.dynamic_slice_in_dim(aperture_end, block_index * W_DEV, W_DEV)
        rate_one = lax.dynamic_slice_in_dim(doppler, block_index * W_DEV, W_DEV)
        rate_two = lax.dynamic_slice_in_dim(chirp_rate, block_index * W_DEV, W_DEV)
        weight_re, weight_im = weights(first_pulse, last_pulse, rate_one, rate_two, pulse_index)
        total = jnp.zeros((2, W_DEV, G), jnp.float32)
        for block_slot in range(2 * REACH + 1):
            low = block_slot * P_DEV
            term = focus_block(weight_re[:, low:low + P_DEV], weight_im[:, low:low + P_DEV], window[:, low:low + P_DEV])
            total = total + settle(term)
        return total
    blocks = lax.map(one_block, jnp.arange(N_SEG, dtype=jnp.int32))
    focused_sum = jnp.transpose(blocks, (1, 0, 2, 3)).reshape(2, WAVES, G)
    power_sum = focused_sum[0] * focused_sum[0] + focused_sum[1] * focused_sum[1]
    power_pad = jnp.pad(power_sum, ((LOOK, LOOK), (0, 0)))
    looked = jnp.zeros((WAVES, G), jnp.float32)
    for shift_row in range(2 * LOOK + 1):
        looked = looked + power_pad[shift_row:shift_row + WAVES]
    multilook = looked / float(2 * LOOK + 1)
    return (focused_sum.astype(jnp.bfloat16), multilook)
```

```python
import functools

import jax
import jax.numpy as jnp
from jax import lax
from jax.experimental import pallas as pl
from jax.experimental.pallas import tpu as pltpu
from jax.sharding import PartitionSpec as P

REACH = 4
LOOK = 8
SHIFT_MAX = 16
F32 = jnp.float32
BF16 = jnp.bfloat16

SIN = (1.0, -0.16666658222675323, 0.008333050645887852, -0.0001980901142815128, 2.605078407214023e-06)
COS = (1.0, -0.5, 0.04166663438081741, -0.0013888359535485506, 2.476008012308739e-05, -2.605002862310357e-07)
PI_HI = 3.140625
PI_LO = 0.0009676536
INV_PI = 0.3183098861837907


PARAMS = pltpu.CompilerParams(vmem_limit_bytes=16 * 2**20)


def neighbour(i, by, odd, devices):
    up = (i // by) % 2 == (1 if odd else 0)
    j = i + by if up else i - by
    return j if 0 <= j < devices else i ^ 1


def swap(array, by, odd):
    devices = lax.axis_size("seg")
    return lax.ppermute(array, "seg", [(i, neighbour(i, by, odd, devices)) for i in range(devices)])


def ring(array):
    devices = lax.axis_size("seg")
    pairs = []
    for i in range(devices):
        j = i + 2 if i % 2 == 0 else i - 2
        pairs.append((i, j if 0 <= j < devices else i ^ 1))
    return lax.ppermute(array, "seg", pairs)


def column(row):
    return jnp.transpose(jnp.broadcast_to(row, (8, row.shape[1])))[:, :1]


def migrate_kernel(pulses_ref, fraction_ref, shift_ref, start_ref, end_ref, doppler_ref, chirp_ref, out_ref, params_ref):
    gates = pulses_ref.shape[2]
    count = pulses_ref.shape[1]
    shape = (count, gates)
    fraction = jnp.broadcast_to(column(fraction_ref[...]), shape)
    shift = jnp.broadcast_to(column(shift_ref[...].astype(F32)), shape).astype(jnp.int32)
    reach = lax.broadcasted_iota(jnp.int32, shape, 1) + shift
    first = jnp.where(reach < gates, 1.0 - fraction, 0.0)
    second = jnp.where(reach + 1 < gates, fraction, 0.0)
    for part in range(2):
        moved = pulses_ref[part].astype(F32)
        bit = 1
        while bit < SHIFT_MAX:
            moved = jnp.where((shift & bit) != 0, pltpu.roll(moved, gates - bit, 1), moved)
            bit *= 2
        out_ref[part] = (first * moved + second * pltpu.roll(moved, gates - 1, 1)).astype(BF16)
    params_ref[0:1, :] = start_ref[...].astype(F32)
    params_ref[1:2, :] = end_ref[...].astype(F32)
    params_ref[2:3, :] = doppler_ref[...]
    params_ref[3:4, :] = chirp_ref[...]
    params_ref[4:8, :] = jnp.zeros((4, params_ref.shape[1]), F32)


def poly(coefs, z):
    total = coefs[-1] * z + coefs[-2]
    for c in coefs[-3::-1]:
        total = total * z + c
    return total


def spread(params_ref, other_ref, cols):
    waves = params_ref.shape[1]
    for half, ref in enumerate((params_ref, other_ref)):
        start, end = ref[0:1, :], ref[1:2, :]
        center = jnp.floor((start + end) * 0.5)
        scale = lax.rsqrt(end - start)
        stack = jnp.concatenate([center, start, end, ref[2:3, :], ref[3:4, :], scale, scale, scale], 0)
        turned = jnp.transpose(stack)
        for k in range(6):
            cols[k, half * waves : (half + 1) * waves, :] = jnp.broadcast_to(turned[:, k : k + 1], (waves, 128))


def weigh(cols, base, pulse_count, rows, put):
    total_rows = cols.shape[1]

    def step(k, carry):
        r = pl.multiple_of(k * rows, rows)
        center, start, end, doppler, chirp, scale = (cols[j, pl.ds(r, rows), :] for j in range(6))
        for lane in range(0, pulse_count, 128):
            pulse = (lax.broadcasted_iota(jnp.int32, (rows, 128), 1) + (base + lane)).astype(F32)
            relative = (pulse - center) * (1.0 / (REACH * pulse_count))
            phase = chirp * relative * relative + doppler * relative
            turns = jnp.round(phase * INV_PI)
            rest = (phase - turns * PI_HI) - turns * PI_LO
            square = rest * rest
            signed = jnp.where((turns.astype(jnp.int32) & 1) != 0, -scale, scale)
            signed = jnp.where((pulse >= start) & (pulse < end), signed, 0.0)
            put(r, lane, signed * poly(COS, square), signed * rest * poly(SIN, square))
        return carry

    lax.fori_loop(0, total_rows // rows, step, 0, unroll=2)


def owner_of(slot, device):
    by, odd = ((2, 0), (2, 1), (4, 0), (4, 1))[slot]
    return jnp.where((device // by) % 2 == odd, device + by, device - by)


def weights_kernel(params_ref, other_ref, own_ref, partial_ref, weights_ref, cols, own_w):
    device = lax.axis_index("seg")
    count = own_ref.shape[1]
    spread(params_ref, other_ref, cols)

    def put_own(r, lane, re, im):
        own_w[0, pl.ds(r, 16), lane : lane + 128] = re.astype(BF16)
        own_w[1, pl.ds(r, 16), lane : lane + 128] = im.astype(BF16)

    weigh(cols, device * count, count, 16, put_own)
    dot = functools.partial(jnp.dot, preferred_element_type=F32)
    partial_ref[0] = dot(own_w[0], own_ref[0]) - dot(own_w[1], own_ref[1])
    partial_ref[1] = dot(own_w[0], own_ref[1]) + dot(own_w[1], own_ref[0])
    for slot in range(4):

        def put(r, lane, re, im, slot=slot):
            weights_ref[0, pl.ds(r, 16), slot * count + lane : slot * count + lane + 128] = re.astype(BF16)
            weights_ref[1, pl.ds(r, 16), slot * count + lane : slot * count + lane + 128] = im.astype(BF16)

        weigh(cols, owner_of(slot, device) * count, count, 16, put)


def focus_kernel(partial_ref, weights_ref, b0, b1, b2, b3, keep_ref, message_ref):
    count = b0.shape[1]
    waves = partial_ref.shape[1] // 2
    dot = functools.partial(jnp.dot, preferred_element_type=F32)
    re, im = partial_ref[0], partial_ref[1]
    minus = jnp.zeros_like(re)
    for slot, ref in enumerate((b0, b1, b2, b3)):
        w_re = weights_ref[0, :, slot * count : (slot + 1) * count]
        w_im = weights_ref[1, :, slot * count : (slot + 1) * count]
        re += dot(w_re, ref[0])
        minus += dot(w_im, ref[1])
        im += dot(w_re, ref[1])
        im += dot(w_im, ref[0])
    re = re - minus
    for part, value in enumerate((re, im)):
        keep_ref[part, :waves] = value[:waves]
        keep_ref[part, waves : waves + LOOK] = value[waves : waves + LOOK]
        keep_ref[part, waves + LOOK :] = value[2 * waves - LOOK :]
        message_ref[part, :waves] = value[waves:].astype(BF16)
        edges = jnp.concatenate([value[:LOOK], value[waves - LOOK : waves]], 0)
        message_ref[part, waves:] = edges.astype(BF16)


def power_kernel(keep_ref, got_ref, focused_ref, looked_ref, edge_ref, ext):
    waves = focused_ref.shape[1]
    core = lax.axis_index("seg") % 2
    total = keep_ref[...] + got_ref[...].astype(F32)
    focused_ref[...] = total[:, :waves].astype(BF16)
    power = total[0] * total[0] + total[1] * total[1]
    initial, last = power[waves : waves + LOOK], power[waves + LOOK :]
    edge_ref[...] = jnp.where(core == 0, last, initial)
    ext[:LOOK] = jnp.where(core == 1, last, 0.0)
    ext[LOOK : LOOK + waves] = power[:waves]
    ext[LOOK + waves :] = jnp.where(core == 0, initial, 0.0)
    rows = waves + 2 * LOOK
    span, window = 1, ext[...]
    while span < 2 * LOOK:
        rows -= span
        window = window[:rows] + window[span : span + rows]
        span *= 2
    looked = window[:waves] + ext[2 * LOOK :]
    looked_ref[...] = looked * (1.0 / (2 * LOOK + 1))


def edge_kernel(devices, looked_ref, edge_ref, out_ref):
    step = pl.program_id(0)
    device = lax.axis_index("seg")
    core = device % 2
    from_chip = device + 4 * core - 2
    here = (step == core) & (from_chip >= 0) & (from_chip < devices)
    scale = jnp.where(here, 1.0 / (2 * LOOK + 1), 0.0)
    row = lax.broadcasted_iota(jnp.int32, edge_ref.shape, 0)
    total = jnp.zeros(edge_ref.shape, F32)
    for h in range(LOOK):
        total += jnp.where((row - h) * (2 * core - 1) >= 0, edge_ref[h : h + 1, :], 0.0)
    out_ref[...] = looked_ref[...] + total * scale


def shards(pulses, fraction, gate_shift, aperture_start, aperture_end, doppler, chirp_rate):
    _, count, gates = pulses.shape
    waves = aperture_start.shape[0]
    devices = lax.axis_size("seg")
    shape = jax.ShapeDtypeStruct
    vmem = pl.BlockSpec(memory_space=pltpu.VMEM)

    migrated, params = pl.pallas_call(
        migrate_kernel,
        out_shape=(shape((2, count, gates), BF16), shape((8, waves), F32)),
        in_specs=[vmem] * 7,
        out_specs=(vmem, vmem),
        compiler_params=PARAMS,
        name="migrate",
    )(
        pulses,
        fraction.reshape(1, count),
        gate_shift.reshape(1, count),
        aperture_start.reshape(1, waves),
        aperture_end.reshape(1, waves),
        doppler.reshape(1, waves),
        chirp_rate.reshape(1, waves),
    )
    blocks = [swap(migrated, by, odd) for by, odd in ((2, 0), (2, 1), (4, 0), (4, 1))]
    other = swap(params, 1, 0)
    partial, weights = pl.pallas_call(
        weights_kernel,
        out_shape=(shape((2, 2 * waves, gates), F32), shape((2, 2 * waves, 4 * count), BF16)),
        in_specs=[vmem] * 3,
        out_specs=(vmem, vmem),
        scratch_shapes=[pltpu.VMEM((6, 2 * waves, 128), F32), pltpu.VMEM((2, 2 * waves, count), BF16)],
        compiler_params=PARAMS,
        name="weights",
    )(params, other, migrated)
    rows = waves + 2 * LOOK
    keep, message = pl.pallas_call(
        focus_kernel,
        out_shape=(shape((2, rows, gates), F32), shape((2, rows, gates), BF16)),
        in_specs=[vmem] * 6,
        out_specs=(vmem, vmem),
        compiler_params=PARAMS,
        name="focus",
    )(partial, weights, *blocks)
    got = swap(message, 1, 0)
    focused, looked, edge = pl.pallas_call(
        power_kernel,
        out_shape=(shape((2, waves, gates), BF16), shape((waves, gates), F32), shape((LOOK, gates), F32)),
        in_specs=[vmem] * 2,
        out_specs=(vmem, vmem, vmem),
        scratch_shapes=[pltpu.VMEM((rows, gates), F32)],
        compiler_params=PARAMS,
        name="power",
    )(keep, got)
    far = ring(edge)
    block = pl.BlockSpec((LOOK, gates), lambda g: (g * (waves // LOOK - 1), 0))
    multilook = pl.pallas_call(
        functools.partial(edge_kernel, devices),
        grid=(2,),
        out_shape=shape((waves, gates), F32),
        in_specs=[block, pl.BlockSpec((LOOK, gates), lambda g: (0, 0))],
        out_specs=block,
        input_output_aliases={0: 0},
        compiler_params=PARAMS,
        name="edge",
    )(looked, far)
    return (focused, multilook)


def solution(mesh):
    part = P(("arcs", "seg"))
    return jax.shard_map(
        shards,
        mesh=mesh,
        in_specs=(P(None, ("arcs", "seg"), None),) + (part,) * 6,
        out_specs=(P(None, ("arcs", "seg"), None), P(("arcs", "seg"), None)),
        check_vma=False,
    )
```

```python
import functools

import jax
import jax.numpy as jnp
from jax import lax
from jax.experimental import pallas as pl
from jax.experimental.pallas import tpu as pltpu
from jax.sharding import PartitionSpec as P


REACH = 4
LOOK = 8
SHIFT_MAX = 16
F32 = jnp.float32
BF16 = jnp.bfloat16

SIN = (1.0, -0.16666658222675323, 0.008333050645887852, -0.0001980901142815128, 2.605078407214023e-06)
COS = (1.0, -0.5, 0.04166663438081741, -0.0013888359535485506, 2.476008012308739e-05, -2.605002862310357e-07)
PI_HI = 3.140625
PI_LO = 0.0009676536
INV_PI = 0.3183098861837907


SLOTS = ((2, 0), (4, 0), (4, 1))
DIAGONAL = (2, 1)
PARAMS = pltpu.CompilerParams(vmem_limit_bytes=16 * 2**20)


def neighbour(i, by, odd, devices):
    up = (i // by) % 2 == (1 if odd else 0)
    j = i + by if up else i - by
    return j if 0 <= j < devices else i ^ 1


def swap(array, by, odd):
    devices = lax.axis_size("seg")
    return lax.ppermute(array, "seg", [(i, neighbour(i, by, odd, devices)) for i in range(devices)])


def beside(array):
    devices = lax.axis_size("seg")
    return lax.ppermute(array, "seg", [(i, (i + 1 if i % 2 else i - 1) % devices) for i in range(devices)])


def column(row):
    return jnp.transpose(jnp.broadcast_to(row, (8, row.shape[1])))[:, :1]


def migrate_kernel(*refs):
    inputs, (out_ref, params_ref), held, sems = refs[:7], refs[7:9], refs[9:16], refs[16]
    copies = [pltpu.make_async_copy(src, dst, sems.at[k]) for k, (src, dst) in enumerate(zip(inputs, held))]
    for copy in copies:
        copy.start()
    for copy in copies[1:]:
        copy.wait()
    pulses_ref, fraction_ref, shift_ref, start_ref, end_ref, doppler_ref, chirp_ref = held
    gates = pulses_ref.shape[2]
    count = pulses_ref.shape[1]
    shape = (count, gates)
    params_ref[0:1, :] = start_ref[...].astype(F32)
    params_ref[1:2, :] = end_ref[...].astype(F32)
    params_ref[2:3, :] = doppler_ref[...]
    params_ref[3:4, :] = chirp_ref[...]
    params_ref[4:8, :] = jnp.zeros((4, params_ref.shape[1]), F32)
    fraction = jnp.broadcast_to(column(fraction_ref[...]), shape)
    shift = jnp.broadcast_to(column(shift_ref[...].astype(F32)), shape).astype(jnp.int32)
    reach = lax.broadcasted_iota(jnp.int32, shape, 1) + shift
    first = jnp.where(reach < gates, 1.0 - fraction, 0.0)
    second = jnp.where(reach + 1 < gates, fraction, 0.0)
    copies[0].wait()
    for part in range(2):
        moved = pulses_ref[part].astype(F32)
        bit = 1
        while bit < SHIFT_MAX:
            moved = jnp.where((shift & bit) != 0, pltpu.roll(moved, gates - bit, 1), moved)
            bit *= 2
        out_ref[part] = (first * moved + second * pltpu.roll(moved, gates - 1, 1)).astype(BF16)


def poly(coefs, z):
    total = coefs[-1] * z + coefs[-2]
    for c in coefs[-3::-1]:
        total = total * z + c
    return total


def spread(refs, cols):
    for at, ref in enumerate(refs):
        waves = ref.shape[1]
        start, end = ref[0:1, :], ref[1:2, :]
        center = jnp.floor((start + end) * 0.5)
        scale = lax.rsqrt(end - start)
        stack = jnp.concatenate([center, start, end, ref[2:3, :], ref[3:4, :], scale, scale, scale], 0)
        turned = jnp.transpose(stack)
        for k in range(6):
            cols[k, at * waves : (at + 1) * waves, :] = jnp.broadcast_to(turned[:, k : k + 1], (waves, 128))


def weigh(cols, base, pulse_count, rows, put):
    total_rows = cols.shape[1]

    def step(k, carry):
        r = pl.multiple_of(k * rows, rows)
        center, start, end, doppler, chirp, scale = (cols[j, pl.ds(r, rows), :] for j in range(6))
        for lane in range(0, pulse_count, 128):
            pulse = (lax.broadcasted_iota(jnp.int32, (rows, 128), 1) + (base + lane)).astype(F32)
            relative = (pulse - center) * (1.0 / (REACH * pulse_count))
            phase = chirp * relative * relative + doppler * relative
            turns = jnp.round(phase * INV_PI)
            rest = (phase - turns * PI_HI) - turns * PI_LO
            square = rest * rest
            signed = jnp.where((turns.astype(jnp.int32) & 1) != 0, -scale, scale)
            signed = jnp.where((pulse >= start) & (pulse < end), signed, 0.0)
            put(r, lane, signed * poly(COS, square), signed * rest * poly(SIN, square))
        return carry

    lax.fori_loop(0, total_rows // rows, step, 0, unroll=2)


def partner(device, by, odd):
    return jnp.where((device // by) % 2 == odd, device + by, device - by)


dot = functools.partial(jnp.dot, preferred_element_type=F32)


def into(ref, at):
    def put(r, lane, re, im):
        ref[0, pl.ds(r, 16), at + lane : at + lane + 128] = re.astype(BF16)
        ref[1, pl.ds(r, 16), at + lane : at + lane + 128] = im.astype(BF16)

    return put


def lend_kernel(target_ref, own_ref, mate_ref, out_ref, cols, w):
    device = lax.axis_index("seg")
    count = own_ref.shape[1]
    mate = device + 1 - 2 * (device % 2)
    spread((target_ref,), cols)
    weigh(cols, device * count, count, 16, into(w, 0))
    weigh(cols, mate * count, count, 16, into(w, count))
    re, im = w[0], w[1]
    a = dot(re[:, :count], own_ref[0]) + dot(re[:, count:], mate_ref[0])
    b = dot(im[:, :count], own_ref[1]) + dot(im[:, count:], mate_ref[1])
    c = dot(re[:, :count], own_ref[1]) + dot(re[:, count:], mate_ref[1])
    d = dot(im[:, :count], own_ref[0]) + dot(im[:, count:], mate_ref[0])
    out_ref[0] = (a - b).astype(BF16)
    out_ref[1] = (c + d).astype(BF16)


def weights_kernel(params_ref, other_ref, own_ref, partial_ref, weights_ref, cols, own_w):
    device = lax.axis_index("seg")
    count = own_ref.shape[1]
    spread((params_ref, other_ref), cols)
    weigh(cols, device * count, count, 16, into(own_w, 0))
    partial_ref[0] = dot(own_w[0], own_ref[0]) - dot(own_w[1], own_ref[1])
    partial_ref[1] = dot(own_w[0], own_ref[1]) + dot(own_w[1], own_ref[0])
    for slot, (by, odd) in enumerate(SLOTS):
        weigh(cols, partner(device, by, odd) * count, count, 16, into(weights_ref, slot * count))


def focus_kernel(partial_ref, weights_ref, *refs):
    blocks, (keep_ref, message_ref) = refs[:-2], refs[-2:]
    count = blocks[0].shape[1]
    waves = keep_ref.shape[1]
    re, im = partial_ref[0], partial_ref[1]
    minus = jnp.zeros_like(re)
    for slot, ref in enumerate(blocks):
        w_re = weights_ref[0, :, slot * count : (slot + 1) * count]
        w_im = weights_ref[1, :, slot * count : (slot + 1) * count]
        re += dot(w_re, ref[0])
        minus += dot(w_im, ref[1])
        im += dot(w_re, ref[1])
        im += dot(w_im, ref[0])
    re = re - minus
    for part, value in enumerate((re, im)):
        keep_ref[part] = value[:waves]
        message_ref[part] = value[waves:].astype(BF16)


def total_of(device, devices, rows, keep_ref, got_ref, lent_ref):
    by_chip = partner(device, *DIAGONAL)
    known = (by_chip >= 0) & (by_chip < devices)
    lent = jnp.where(known, lent_ref[:, rows].astype(F32), 0.0)
    return keep_ref[:, rows] + got_ref[:, rows].astype(F32) + lent


def ends_kernel(devices, keep_ref, got_ref, lent_ref, near_ref, far_ref):
    device = lax.axis_index("seg")
    waves = keep_ref.shape[1]
    powers = []
    for rows in (slice(0, 2 * LOOK), slice(waves - 2 * LOOK, waves)):
        total = total_of(device, devices, rows, keep_ref, got_ref, lent_ref)
        powers.append(total[0] * total[0] + total[1] * total[1])
    initial, last = powers[0][:LOOK], powers[1][LOOK:]
    core = device % 2
    near_ref[...] = jnp.where(core == 0, last, initial)
    far_ref[...] = jnp.where(core == 0, initial, last)


def power_kernel(devices, keep_ref, got_ref, lent_ref, focused_ref, looked_ref, ends_ref, ext):
    waves = focused_ref.shape[1]
    total = total_of(lax.axis_index("seg"), devices, slice(0, waves), keep_ref, got_ref, lent_ref)
    focused_ref[...] = total.astype(BF16)
    ext[:LOOK] = jnp.zeros((LOOK, ext.shape[1]), F32)
    ext[LOOK : LOOK + waves] = total[0] * total[0] + total[1] * total[1]
    ext[LOOK + waves :] = jnp.zeros((LOOK, ext.shape[1]), F32)
    rows = waves + 2 * LOOK
    span, window = 1, ext[...]
    while span < 2 * LOOK:
        rows -= span
        window = window[:rows] + window[span : span + rows]
        span *= 2
    looked = (window[:waves] + ext[2 * LOOK :]) * (1.0 / (2 * LOOK + 1))
    looked_ref[...] = looked
    ends_ref[:LOOK] = looked[:LOOK]
    ends_ref[LOOK:] = looked[waves - LOOK :]


def edge_kernel(devices, looked_ref, ends_ref, near_ref, far_ref, out_ref, rows, sems):
    device = lax.axis_index("seg")
    core = device % 2
    beside = device + 2 * core - 1
    scale = 1.0 / (2 * LOOK + 1)
    near = near_ref[...] * scale
    far = far_ref[...] * jnp.where((beside >= 0) & (beside < devices), scale, 0.0)
    row = lax.broadcasted_iota(jnp.int32, near.shape, 0)
    before, after = jnp.where(core == 0, far, near), jnp.where(core == 0, near, far)
    top, bottom = ends_ref[:LOOK], ends_ref[LOOK:]
    for h in range(LOOK):
        top += jnp.where(row <= h, before[h : h + 1, :], 0.0)
        bottom += jnp.where(row >= h, after[h : h + 1, :], 0.0)
    rows[0] = top
    rows[1] = bottom
    waves = out_ref.shape[0]
    copies = [
        pltpu.make_async_copy(rows.at[k], out_ref.at[pl.ds(at, LOOK)], sems.at[k])
        for k, at in enumerate((0, waves - LOOK))
    ]
    for copy in copies:
        copy.start()
    for copy in copies:
        copy.wait()


def shards(pulses, fraction, gate_shift, aperture_start, aperture_end, doppler, chirp_rate):
    _, count, gates = pulses.shape
    waves = aperture_start.shape[0]
    devices = lax.axis_size("seg")
    shape = jax.ShapeDtypeStruct
    vmem = pl.BlockSpec(memory_space=pltpu.VMEM)
    hbm = pl.BlockSpec(memory_space=pltpu.HBM)

    inputs = (
        pulses,
        fraction.reshape(1, count),
        gate_shift.reshape(1, count),
        aperture_start.reshape(1, waves),
        aperture_end.reshape(1, waves),
        doppler.reshape(1, waves),
        chirp_rate.reshape(1, waves),
    )
    migrated, params = pl.pallas_call(
        migrate_kernel,
        out_shape=(shape((2, count, gates), BF16), shape((8, waves), F32)),
        in_specs=[hbm] * 7,
        out_specs=(vmem, vmem),
        scratch_shapes=[pltpu.VMEM(a.shape, a.dtype) for a in inputs] + [pltpu.SemaphoreType.DMA((7,))],
        compiler_params=PARAMS,
        name="migrate",
    )(*(pltpu.with_memory_space_constraint(a, pltpu.HBM) for a in inputs))
    blocks = [swap(migrated, by, odd) for by, odd in SLOTS]
    target = swap(params, *DIAGONAL)
    mate = swap(migrated, 1, 0)
    other = swap(params, 1, 0)
    lending = pl.pallas_call(
        lend_kernel,
        out_shape=shape((2, waves, gates), BF16),
        in_specs=[vmem] * 3,
        out_specs=vmem,
        scratch_shapes=[pltpu.VMEM((6, waves, 128), F32), pltpu.VMEM((2, waves, 2 * count), BF16)],
        compiler_params=PARAMS,
        name="lend",
    )(target, migrated, mate)
    lent = swap(lending, *DIAGONAL)
    partial, weights = pl.pallas_call(
        weights_kernel,
        out_shape=(shape((2, 2 * waves, gates), F32), shape((2, 2 * waves, len(SLOTS) * count), BF16)),
        in_specs=[vmem] * 3,
        out_specs=(vmem, vmem),
        scratch_shapes=[pltpu.VMEM((6, 2 * waves, 128), F32), pltpu.VMEM((2, 2 * waves, count), BF16)],
        compiler_params=PARAMS,
        name="weights",
    )(params, other, migrated)
    keep, message = pl.pallas_call(
        focus_kernel,
        out_shape=(shape((2, waves, gates), F32), shape((2, waves, gates), BF16)),
        in_specs=[vmem] * (2 + len(blocks)),
        out_specs=(vmem, vmem),
        compiler_params=PARAMS,
        name="focus",
    )(partial, weights, *blocks)
    got = swap(message, 1, 0)
    near, far = pl.pallas_call(
        functools.partial(ends_kernel, devices),
        out_shape=(shape((LOOK, gates), F32),) * 2,
        in_specs=[vmem] * 3,
        out_specs=(vmem, vmem),
        compiler_params=PARAMS,
        name="ends",
    )(keep, got, lent)
    far = beside(far)
    near = swap(near, 1, 0)
    focused, looked, ends = pl.pallas_call(
        functools.partial(power_kernel, devices),
        out_shape=(shape((2, waves, gates), BF16), shape((waves, gates), F32), shape((2 * LOOK, gates), F32)),
        in_specs=[vmem] * 3,
        out_specs=(vmem, vmem, vmem),
        scratch_shapes=[pltpu.VMEM((waves + 2 * LOOK, gates), F32)],
        compiler_params=PARAMS,
        name="power",
    )(keep, got, lent)
    multilook = pl.pallas_call(
        functools.partial(edge_kernel, devices),
        out_shape=shape((waves, gates), F32),
        in_specs=[hbm, vmem, vmem, vmem],
        out_specs=hbm,
        scratch_shapes=[pltpu.VMEM((2, LOOK, gates), F32), pltpu.SemaphoreType.DMA((2,))],
        input_output_aliases={0: 0},
        compiler_params=PARAMS,
        name="edge",
    )(looked, ends, near, far)
    return (focused, multilook)


def solution(mesh):
    part = P(("arcs", "seg"))
    return jax.shard_map(
        shards,
        mesh=mesh,
        in_specs=(P(None, ("arcs", "seg"), None),) + (part,) * 6,
        out_specs=(P(None, ("arcs", "seg"), None), P(("arcs", "seg"), None)),
        check_vma=False,
    )
```

```python
import functools
import math

import jax
import jax.numpy as jnp
from jax import lax
from jax.experimental import pallas as pl
from jax.experimental.pallas import tpu as pltpu
from jax.sharding import PartitionSpec as P


REACH = 4
LOOK = 8
F32 = jnp.float32
BF16 = jnp.bfloat16

SIN = (3.1415927410125732, -5.167710304260254, 2.550077438354492, -0.5982902646064758, 0.07765503972768784)
COS = (0.9999999403953552, -4.934792995452881, 4.058411121368408, -1.3318735361099243, 0.21968165040016174)
SLOTS = ((2, 0), (4, 0), (4, 1))
DIAGONAL = (2, 1)
PARAMS = pltpu.CompilerParams(vmem_limit_bytes=16 * 2**20)


def neighbour(i, by, odd, devices):
    up = (i // by) % 2 == (1 if odd else 0)
    j = i + by if up else i - by
    return j if 0 <= j < devices else i ^ 1


def swap(array, by, odd):
    devices = lax.axis_size("seg")
    return lax.ppermute(array, "seg", [(i, neighbour(i, by, odd, devices)) for i in range(devices)])


def beside(array):
    arcs, devices = lax.axis_size("arcs"), lax.axis_size("seg")
    pairs = []
    for arc in range(arcs):
        for i in range(devices):
            j = i + 1 if i % 2 else i - 1
            to = (arc, j) if 0 <= j < devices else (arc ^ 1, i) if arcs % 2 == 0 else (arc, j % devices)
            pairs.append((arc * devices + i, to[0] * devices + to[1]))
    return lax.ppermute(array, ("arcs", "seg"), pairs)


def migrate_kernel(*refs):
    inputs, (out_ref, params_ref), held, (turned, sems) = refs[:7], refs[7:9], refs[9:16], refs[16:]
    copies = [pltpu.make_async_copy(src, dst, sems.at[k]) for k, (src, dst) in enumerate(zip(inputs, held))]
    for copy in copies:
        copy.start()
    for copy in copies[1:]:
        copy.wait()
    pulses_ref, fraction_ref, shift_ref, start_ref, end_ref, doppler_ref, chirp_ref = held
    _, count, gates = pulses_ref.shape
    params_ref[0:1, :] = start_ref[...].astype(F32)
    params_ref[1:2, :] = end_ref[...].astype(F32)
    params_ref[2:3, :] = doppler_ref[...]
    params_ref[3:4, :] = chirp_ref[...]
    params_ref[4:8, :] = jnp.zeros((4, params_ref.shape[1]), F32)
    spare = jnp.zeros((6, count), F32)
    turned[...] = jnp.transpose(jnp.concatenate([fraction_ref[...], shift_ref[...].astype(F32), spare], 0))
    copies[0].wait()
    rows = 64
    lane = lax.broadcasted_iota(jnp.int32, (rows, 128), 1)
    pick = functools.partial(jnp.take_along_axis, axis=1, mode="promise_in_bounds")
    for r in range(0, count, rows):
        fraction = jnp.broadcast_to(turned[r : r + rows, 0:1], (rows, 128))
        shift = jnp.broadcast_to(turned[r : r + rows, 1:2], (rows, 128)).astype(jnp.int32)
        terms = [(by, (lane + by) & 127, part) for by, part in ((shift, 1.0 - fraction), (shift + 1, fraction))]
        for part in range(2):
            tiles = [pulses_ref[part, r : r + rows, at : at + 128].astype(F32) for at in range(0, gates, 128)]
            total = [0.0] * len(tiles)
            for by, at, scale in terms:
                inside = lane + by < 128
                moved = [pick(t, at) for t in tiles] + [0.0]
                for j in range(len(tiles)):
                    total[j] += scale * jnp.where(inside, moved[j], moved[j + 1])
            for j, value in enumerate(total):
                out_ref[part, r : r + rows, j * 128 : (j + 1) * 128] = value.astype(BF16)


def poly(coefs, z):
    total = coefs[-1] * z + coefs[-2]
    for c in coefs[-3::-1]:
        total = total * z + c
    return total


def spread(ref, reach, cols):
    waves = ref.shape[1]
    start, end = ref[0:1, :], ref[1:2, :]
    center = jnp.floor((start + end) * 0.5)
    linear = ref[2:3, :] * (1.0 / (math.pi * reach))
    square = ref[3:4, :] * (1.0 / (math.pi * reach * reach))
    scale = lax.rsqrt(end - start)
    turned = jnp.transpose(jnp.concatenate([center, start, end, linear, square, scale, scale, scale], 0))
    for k in range(6):
        cols[k] = jnp.broadcast_to(turned[:, k : k + 1], (waves, 128))


def weigh(cols, base, pulse_count, put, rows=16, unroll=2):
    lanes = range(0, pulse_count, 128)
    at = lax.broadcasted_iota(jnp.int32, (rows, 128), 1) + base
    pulses = [(at + lane).astype(F32) for lane in lanes]

    def step(k, carry):
        r = pl.multiple_of(k * rows, rows)
        center, start, end, linear, square, scale = (cols[j, pl.ds(r, rows), :] for j in range(6))
        minus = -scale
        for lane, pulse in zip(lanes, pulses):
            u = pulse - center
            halves = (square * u + linear) * u
            near = jnp.round(halves)
            rest = halves - near
            z = rest * rest
            signed = jnp.where((near.astype(jnp.int32) & 1) != 0, minus, scale)
            signed = jnp.where((pulse >= start) & (pulse < end), signed, 0.0)
            put(r, lane, signed * poly(COS, z), signed * rest * poly(SIN, z))
        return carry

    lax.fori_loop(0, cols.shape[1] // rows, step, 0, unroll=unroll)


def partner(device, by, odd):
    return jnp.where((device // by) % 2 == odd, device + by, device - by)


dot = functools.partial(jnp.dot, preferred_element_type=F32)


def into(ref, at):
    def put(r, lane, re, im):
        ref[0, pl.ds(r, 16), at + lane : at + lane + 128] = re.astype(BF16)
        ref[1, pl.ds(r, 16), at + lane : at + lane + 128] = im.astype(BF16)

    return put


def lend_kernel(target_ref, own_ref, mate_ref, out_ref, cols, w):
    device = lax.axis_index("seg")
    count = own_ref.shape[1]
    mate = device + 1 - 2 * (device % 2)
    spread(target_ref, REACH * count, cols)
    weigh(cols, device * count, count, into(w, 0))
    weigh(cols, mate * count, count, into(w, count))
    re, im = w[0], w[1]
    a = dot(re[:, :count], own_ref[0]) + dot(re[:, count:], mate_ref[0])
    b = dot(im[:, :count], own_ref[1]) + dot(im[:, count:], mate_ref[1])
    c = dot(re[:, :count], own_ref[1]) + dot(re[:, count:], mate_ref[1])
    d = dot(im[:, :count], own_ref[0]) + dot(im[:, count:], mate_ref[0])
    out_ref[0] = (a - b).astype(BF16)
    out_ref[1] = (c + d).astype(BF16)


def weights_kernel(params_ref, own_ref, partial_ref, weights_ref, cols, own_w):
    device = lax.axis_index("seg")
    count = own_ref.shape[1]
    spread(params_ref, REACH * count, cols)
    weigh(cols, device * count, count, into(own_w, 0))
    partial_ref[0] = dot(own_w[0], own_ref[0]) - dot(own_w[1], own_ref[1])
    partial_ref[1] = dot(own_w[0], own_ref[1]) + dot(own_w[1], own_ref[0])
    for slot, (by, odd) in enumerate(SLOTS):
        weigh(cols, partner(device, by, odd) * count, count, into(weights_ref, slot * count))


def focus_kernel(partial_ref, weights_ref, partial2_ref, weights2_ref, *refs):
    blocks, (keep_ref, message_ref) = refs[:-2], refs[-2:]
    count = blocks[0].shape[1]
    for p_ref, w_ref, out in ((partial2_ref, weights2_ref, message_ref), (partial_ref, weights_ref, keep_ref)):
        re, im = p_ref[0], p_ref[1]
        minus = jnp.zeros_like(re)
        for slot, ref in enumerate(blocks):
            w_re = w_ref[0, :, slot * count : (slot + 1) * count]
            w_im = w_ref[1, :, slot * count : (slot + 1) * count]
            re += dot(w_re, ref[0])
            minus += dot(w_im, ref[1])
            im += dot(w_re, ref[1])
            im += dot(w_im, ref[0])
        out[0] = (re - minus).astype(out.dtype)
        out[1] = im.astype(out.dtype)


def total_of(device, devices, rows, keep_ref, got_ref, lent_ref):
    by_chip = partner(device, *DIAGONAL)
    known = (by_chip >= 0) & (by_chip < devices)
    lent = jnp.where(known, lent_ref[:, rows].astype(F32), 0.0)
    return keep_ref[:, rows] + got_ref[:, rows].astype(F32) + lent


def ends_kernel(devices, keep_ref, got_ref, lent_ref, near_ref, far_ref):
    device = lax.axis_index("seg")
    waves = keep_ref.shape[1]
    powers = []
    for rows in (slice(0, 2 * LOOK), slice(waves - 2 * LOOK, waves)):
        total = total_of(device, devices, rows, keep_ref, got_ref, lent_ref)
        powers.append(total[0] * total[0] + total[1] * total[1])
    initial, last = powers[0][:LOOK], powers[1][LOOK:]
    core = device % 2
    near_ref[...] = jnp.where(core == 0, last, initial)
    far_ref[...] = jnp.where(core == 0, initial, last)


def power_kernel(devices, keep_ref, got_ref, lent_ref, focused_ref, looked_ref, ends_ref, ext):
    waves = focused_ref.shape[1]
    total = total_of(lax.axis_index("seg"), devices, slice(0, waves), keep_ref, got_ref, lent_ref)
    focused_ref[...] = total.astype(BF16)
    ext[:LOOK] = jnp.zeros((LOOK, ext.shape[1]), F32)
    ext[LOOK : LOOK + waves] = total[0] * total[0] + total[1] * total[1]
    ext[LOOK + waves :] = jnp.zeros((LOOK, ext.shape[1]), F32)
    rows = waves + 2 * LOOK
    span, window = 1, ext[...]
    while span < 2 * LOOK:
        rows -= span
        window = window[:rows] + window[span : span + rows]
        span *= 2
    looked = (window[:waves] + ext[2 * LOOK :]) * (1.0 / (2 * LOOK + 1))
    looked_ref[...] = looked
    ends_ref[:LOOK] = looked[:LOOK]
    ends_ref[LOOK:] = looked[waves - LOOK :]


def edge_kernel(devices, looked_ref, ends_ref, near_ref, far_ref, out_ref, rows, sems):
    device = lax.axis_index("seg")
    core = device % 2
    beside = device + 2 * core - 1
    scale = 1.0 / (2 * LOOK + 1)
    near = near_ref[...] * scale
    far = far_ref[...] * jnp.where((beside >= 0) & (beside < devices), scale, 0.0)
    row = lax.broadcasted_iota(jnp.int32, near.shape, 0)
    before, after = jnp.where(core == 0, far, near), jnp.where(core == 0, near, far)
    top, bottom = ends_ref[:LOOK], ends_ref[LOOK:]
    for h in range(LOOK):
        top += jnp.where(row <= h, before[h : h + 1, :], 0.0)
        bottom += jnp.where(row >= h, after[h : h + 1, :], 0.0)
    rows[0] = top
    rows[1] = bottom
    waves = out_ref.shape[0]
    copies = [
        pltpu.make_async_copy(rows.at[k], out_ref.at[pl.ds(at, LOOK)], sems.at[k])
        for k, at in enumerate((0, waves - LOOK))
    ]
    for copy in copies:
        copy.start()
    for copy in copies:
        copy.wait()


def shards(pulses, fraction, gate_shift, aperture_start, aperture_end, doppler, chirp_rate):
    _, count, gates = pulses.shape
    waves = aperture_start.shape[0]
    devices = lax.axis_size("seg")
    shape = jax.ShapeDtypeStruct
    vmem = pl.BlockSpec(memory_space=pltpu.VMEM)
    hbm = pl.BlockSpec(memory_space=pltpu.HBM)

    inputs = (
        pulses,
        fraction.reshape(1, count),
        gate_shift.reshape(1, count),
        aperture_start.reshape(1, waves),
        aperture_end.reshape(1, waves),
        doppler.reshape(1, waves),
        chirp_rate.reshape(1, waves),
    )
    migrated, params = pl.pallas_call(
        migrate_kernel,
        out_shape=(shape((2, count, gates), BF16), shape((8, waves), F32)),
        in_specs=[hbm] * 7,
        out_specs=(vmem, vmem),
        scratch_shapes=[pltpu.VMEM(a.shape, a.dtype) for a in inputs] + [pltpu.VMEM((count, 8), F32), pltpu.SemaphoreType.DMA((7,))],
        compiler_params=PARAMS,
        name="migrate",
    )(*(pltpu.with_memory_space_constraint(a, pltpu.HBM) for a in inputs))
    blocks = [swap(migrated, by, odd) for by, odd in SLOTS]
    target = swap(params, *DIAGONAL)
    mate = swap(migrated, 1, 0)
    other = swap(params, 1, 0)
    lending = pl.pallas_call(
        lend_kernel,
        out_shape=shape((2, waves, gates), BF16),
        in_specs=[vmem] * 3,
        out_specs=vmem,
        scratch_shapes=[pltpu.VMEM((6, waves, 128), F32), pltpu.VMEM((2, waves, 2 * count), BF16)],
        compiler_params=PARAMS,
        name="lend",
    )(target, migrated, mate)
    lent = swap(lending, *DIAGONAL)
    weigh_call = lambda: pl.pallas_call(
        weights_kernel,
        out_shape=(shape((2, waves, gates), F32), shape((2, waves, len(SLOTS) * count), BF16)),
        in_specs=[vmem] * 2,
        out_specs=(vmem, vmem),
        scratch_shapes=[pltpu.VMEM((6, waves, 128), F32), pltpu.VMEM((2, waves, count), BF16)],
        compiler_params=PARAMS,
    )
    partial, weights = weigh_call()(params, migrated)
    partial2, weights2 = weigh_call()(other, migrated)
    keep, message = pl.pallas_call(
        focus_kernel,
        out_shape=(shape((2, waves, gates), F32), shape((2, waves, gates), BF16)),
        in_specs=[vmem] * (4 + len(blocks)),
        out_specs=(vmem, vmem),
        compiler_params=PARAMS,
        name="focus",
    )(partial, weights, partial2, weights2, *blocks)
    got = swap(message, 1, 0)
    near, far = pl.pallas_call(
        functools.partial(ends_kernel, devices),
        out_shape=(shape((LOOK, gates), F32),) * 2,
        in_specs=[vmem] * 3,
        out_specs=(vmem, vmem),
        compiler_params=PARAMS,
        name="ends",
    )(keep, got, lent)
    far = beside(far)
    near = swap(near, 1, 0)
    focused, looked, ends = pl.pallas_call(
        functools.partial(power_kernel, devices),
        out_shape=(shape((2, waves, gates), BF16), shape((waves, gates), F32), shape((2 * LOOK, gates), F32)),
        in_specs=[vmem] * 3,
        out_specs=(vmem, vmem, vmem),
        scratch_shapes=[pltpu.VMEM((waves + 2 * LOOK, gates), F32)],
        compiler_params=PARAMS,
        name="power",
    )(keep, got, lent)
    multilook = pl.pallas_call(
        functools.partial(edge_kernel, devices),
        out_shape=shape((waves, gates), F32),
        in_specs=[hbm, vmem, vmem, vmem],
        out_specs=hbm,
        scratch_shapes=[pltpu.VMEM((2, LOOK, gates), F32), pltpu.SemaphoreType.DMA((2,))],
        input_output_aliases={0: 0},
        compiler_params=PARAMS,
        name="edge",
    )(looked, ends, near, far)
    return (focused, multilook)


def solution(mesh):
    part = P(("arcs", "seg"))
    return jax.shard_map(
        shards,
        mesh=mesh,
        in_specs=(P(None, ("arcs", "seg"), None),) + (part,) * 6,
        out_specs=(P(None, ("arcs", "seg"), None), P(("arcs", "seg"), None)),
        check_vma=False,
    )
```

```python
import functools
import math

import jax
import jax.numpy as jnp
from jax import lax
from jax.experimental import pallas as pl
from jax.experimental.pallas import tpu as pltpu
from jax.sharding import PartitionSpec as P


REACH = 4
LOOK = 8
F32 = jnp.float32
BF16 = jnp.bfloat16

SIN = (3.1415927410125732, -5.167710304260254, 2.550077438354492, -0.5982902646064758, 0.07765503972768784)
COS = (0.9999999403953552, -4.934792995452881, 4.058411121368408, -1.3318735361099243, 0.21968165040016174)
SLOTS = ((2, 0), (4, 0), (4, 1))
DIAGONAL = (2, 1)
PARAMS = pltpu.CompilerParams(vmem_limit_bytes=16 * 2**20)


def neighbour(i, by, odd, devices):
    up = (i // by) % 2 == (1 if odd else 0)
    j = i + by if up else i - by
    return j if 0 <= j < devices else i ^ 1


def swap(array, by, odd):
    devices = lax.axis_size("seg")
    return lax.ppermute(array, "seg", [(i, neighbour(i, by, odd, devices)) for i in range(devices)])


def beside(array):
    arcs, devices = lax.axis_size("arcs"), lax.axis_size("seg")
    pairs = []
    for arc in range(arcs):
        for i in range(devices):
            j = i + 1 if i % 2 else i - 1
            to = (arc, j) if 0 <= j < devices else (arc ^ 1, i) if arcs % 2 == 0 else (arc, j % devices)
            pairs.append((arc * devices + i, to[0] * devices + to[1]))
    return lax.ppermute(array, ("arcs", "seg"), pairs)


def migrate_kernel(*refs):
    inputs, (out_ref, params_ref), held, (turned, sems) = refs[:7], refs[7:9], refs[9:16], refs[16:]
    copies = [pltpu.make_async_copy(src, dst, sems.at[k]) for k, (src, dst) in enumerate(zip(inputs, held))]
    for copy in copies:
        copy.start()
    for copy in copies[1:]:
        copy.wait()
    pulses_ref, fraction_ref, shift_ref, start_ref, end_ref, doppler_ref, chirp_ref = held
    _, count, gates = pulses_ref.shape
    params_ref[0:1, :] = start_ref[...].astype(F32)
    params_ref[1:2, :] = end_ref[...].astype(F32)
    params_ref[2:3, :] = doppler_ref[...]
    params_ref[3:4, :] = chirp_ref[...]
    params_ref[4:8, :] = jnp.zeros((4, params_ref.shape[1]), F32)
    spare = jnp.zeros((6, count), F32)
    turned[...] = jnp.transpose(jnp.concatenate([fraction_ref[...], shift_ref[...].astype(F32), spare], 0))
    copies[0].wait()
    rows = 64
    lane = lax.broadcasted_iota(jnp.int32, (rows, 128), 1)
    pick = functools.partial(jnp.take_along_axis, axis=1, mode="promise_in_bounds")
    for r in range(0, count, rows):
        fraction = jnp.broadcast_to(turned[r : r + rows, 0:1], (rows, 128))
        shift = jnp.broadcast_to(turned[r : r + rows, 1:2], (rows, 128)).astype(jnp.int32)
        terms = [(by, (lane + by) & 127, part) for by, part in ((shift, 1.0 - fraction), (shift + 1, fraction))]
        for part in range(2):
            tiles = [pulses_ref[part, r : r + rows, at : at + 128].astype(F32) for at in range(0, gates, 128)]
            total = [0.0] * len(tiles)
            for by, at, scale in terms:
                inside = lane + by < 128
                moved = [pick(t, at) for t in tiles] + [0.0]
                for j in range(len(tiles)):
                    total[j] += scale * jnp.where(inside, moved[j], moved[j + 1])
            for j, value in enumerate(total):
                out_ref[part, r : r + rows, j * 128 : (j + 1) * 128] = value.astype(BF16)


def poly(coefs, z):
    total = coefs[-1] * z + coefs[-2]
    for c in coefs[-3::-1]:
        total = total * z + c
    return total


def spread(ref, reach, cols):
    waves = ref.shape[1]
    start, end = ref[0:1, :], ref[1:2, :]
    center = jnp.floor((start + end) * 0.5)
    linear = ref[2:3, :] * (1.0 / (math.pi * reach))
    square = ref[3:4, :] * (1.0 / (math.pi * reach * reach))
    scale = lax.rsqrt(end - start)
    turned = jnp.transpose(jnp.concatenate([center, start, end, linear, square, scale, scale, scale], 0))
    for k in range(6):
        cols[k] = jnp.broadcast_to(turned[:, k : k + 1], (waves, 128))


def weigh(cols, base, pulse_count, put, rows=16, unroll=8):
    lanes = range(0, pulse_count, 128)
    at = lax.broadcasted_iota(jnp.int32, (rows, 128), 1) + base
    pulses = [(at + lane).astype(F32) for lane in lanes]

    def step(k, carry):
        r = pl.multiple_of(k * rows, rows)
        center, start, end, linear, square, scale = (cols[j, pl.ds(r, rows), :] for j in range(6))
        minus = -scale
        for lane, pulse in zip(lanes, pulses):
            u = pulse - center
            halves = (square * u + linear) * u
            near = jnp.round(halves)
            rest = halves - near
            z = rest * rest
            signed = jnp.where((near.astype(jnp.int32) & 1) != 0, minus, scale)
            signed = jnp.where((pulse >= start) & (pulse < end), signed, 0.0)
            put(r, lane, signed * poly(COS, z), signed * rest * poly(SIN, z))
        return carry

    lax.fori_loop(0, cols.shape[1] // rows, step, 0, unroll=unroll)


def partner(device, by, odd):
    return jnp.where((device // by) % 2 == odd, device + by, device - by)


dot = functools.partial(jnp.dot, preferred_element_type=F32)


def into(ref, at):
    def put(r, lane, re, im):
        ref[0, pl.ds(r, 16), at + lane : at + lane + 128] = re.astype(BF16)
        ref[1, pl.ds(r, 16), at + lane : at + lane + 128] = im.astype(BF16)

    return put


def lend_weights_kernel(target_ref, out_ref, cols):
    device = lax.axis_index("seg")
    count = out_ref.shape[2] // 2
    mate = device + 1 - 2 * (device % 2)
    spread(target_ref, REACH * count, cols)
    weigh(cols, device * count, count, into(out_ref, 0))
    weigh(cols, mate * count, count, into(out_ref, count))


def lend_kernel(w_ref, own_ref, mate_ref, out_ref, ends_ref):
    count = own_ref.shape[1]
    waves = out_ref.shape[1]
    re, im = w_ref[0], w_ref[1]
    a = dot(re[:, :count], own_ref[0]) + dot(re[:, count:], mate_ref[0])
    b = dot(im[:, :count], own_ref[1]) + dot(im[:, count:], mate_ref[1])
    c = dot(re[:, :count], own_ref[1]) + dot(re[:, count:], mate_ref[1])
    d = dot(im[:, :count], own_ref[0]) + dot(im[:, count:], mate_ref[0])
    for part, value in enumerate((a - b, c + d)):
        out_ref[part] = value.astype(BF16)
        ends_ref[part] = jnp.concatenate([value[:LOOK], value[waves - LOOK :]], 0).astype(BF16)


def weights_kernel(params_ref, own_ref, partial_ref, weights_ref, cols, own_w):
    device = lax.axis_index("seg")
    count = own_ref.shape[1]
    spread(params_ref, REACH * count, cols)
    weigh(cols, device * count, count, into(own_w, 0))
    partial_ref[0] = dot(own_w[0], own_ref[0]) - dot(own_w[1], own_ref[1])
    partial_ref[1] = dot(own_w[0], own_ref[1]) + dot(own_w[1], own_ref[0])
    for slot, (by, odd) in enumerate(SLOTS):
        weigh(cols, partner(device, by, odd) * count, count, into(weights_ref, slot * count))


def focus_kernel(partial_ref, weights_ref, *refs):
    blocks, out_ref = refs[:-1], refs[-1]
    count = blocks[0].shape[1]
    re, im = partial_ref[0], partial_ref[1]
    minus = jnp.zeros_like(re)
    for slot, ref in enumerate(blocks):
        w_re = weights_ref[0, :, slot * count : (slot + 1) * count]
        w_im = weights_ref[1, :, slot * count : (slot + 1) * count]
        re += dot(w_re, ref[0])
        minus += dot(w_im, ref[1])
        im += dot(w_re, ref[1])
        im += dot(w_im, ref[0])
    out_ref[0] = (re - minus).astype(out_ref.dtype)
    out_ref[1] = im.astype(out_ref.dtype)


def total_of(devices, keep, got, lent):
    by_chip = partner(lax.axis_index("seg"), *DIAGONAL)
    known = (by_chip >= 0) & (by_chip < devices)
    return keep + got.astype(F32) + jnp.where(known, lent.astype(F32), 0.0)


def ends_kernel(devices, keep_ref, got_ref, lent_ref, near_ref, far_ref):
    waves = keep_ref.shape[1]
    pair = slice(0, 2 * LOOK), slice(waves - 2 * LOOK, waves)
    keep, got = (
        jnp.concatenate([ref[:, pair[0]].astype(F32)[:, :LOOK], ref[:, pair[1]].astype(F32)[:, LOOK:]], 1)
        for ref in (keep_ref, got_ref)
    )
    total = total_of(devices, keep, got, lent_ref[...])
    power = total[0] * total[0] + total[1] * total[1]
    initial, last = power[:LOOK], power[LOOK:]
    core = lax.axis_index("seg") % 2
    near_ref[...] = jnp.where(core == 0, last, initial)
    far_ref[...] = jnp.where(core == 0, initial, last)


def power_kernel(devices, keep_ref, got_ref, lent_ref, focused_ref, looked_ref, ends_ref, ext):
    waves = focused_ref.shape[1]
    total = total_of(devices, keep_ref[...], got_ref[...], lent_ref[...])
    focused_ref[...] = total.astype(BF16)
    ext[:LOOK] = jnp.zeros((LOOK, ext.shape[1]), F32)
    ext[LOOK : LOOK + waves] = total[0] * total[0] + total[1] * total[1]
    ext[LOOK + waves :] = jnp.zeros((LOOK, ext.shape[1]), F32)
    rows = waves + 2 * LOOK
    span, window = 1, ext[...]
    while span < 2 * LOOK:
        rows -= span
        window = window[:rows] + window[span : span + rows]
        span *= 2
    looked = (window[:waves] + ext[2 * LOOK :]) * (1.0 / (2 * LOOK + 1))
    looked_ref[...] = looked
    ends_ref[:LOOK] = looked[:LOOK]
    ends_ref[LOOK:] = looked[waves - LOOK :]


def edge_kernel(devices, looked_ref, ends_ref, near_ref, far_ref, out_ref, rows, sems):
    device = lax.axis_index("seg")
    core = device % 2
    beside = device + 2 * core - 1
    scale = 1.0 / (2 * LOOK + 1)
    near = near_ref[...] * scale
    far = far_ref[...] * jnp.where((beside >= 0) & (beside < devices), scale, 0.0)
    row = lax.broadcasted_iota(jnp.int32, near.shape, 0)
    before, after = jnp.where(core == 0, far, near), jnp.where(core == 0, near, far)
    top, bottom = ends_ref[:LOOK], ends_ref[LOOK:]
    for h in range(LOOK):
        top += jnp.where(row <= h, before[h : h + 1, :], 0.0)
        bottom += jnp.where(row >= h, after[h : h + 1, :], 0.0)
    rows[0] = top
    rows[1] = bottom
    waves = out_ref.shape[0]
    copies = [
        pltpu.make_async_copy(rows.at[k], out_ref.at[pl.ds(at, LOOK)], sems.at[k])
        for k, at in enumerate((0, waves - LOOK))
    ]
    for copy in copies:
        copy.start()
    for copy in copies:
        copy.wait()


def shards(pulses, fraction, gate_shift, aperture_start, aperture_end, doppler, chirp_rate):
    _, count, gates = pulses.shape
    waves = aperture_start.shape[0]
    devices = lax.axis_size("seg")
    shape = jax.ShapeDtypeStruct
    vmem = pl.BlockSpec(memory_space=pltpu.VMEM)
    hbm = pl.BlockSpec(memory_space=pltpu.HBM)

    inputs = (
        pulses,
        fraction.reshape(1, count),
        gate_shift.reshape(1, count),
        aperture_start.reshape(1, waves),
        aperture_end.reshape(1, waves),
        doppler.reshape(1, waves),
        chirp_rate.reshape(1, waves),
    )
    migrated, params = pl.pallas_call(
        migrate_kernel,
        out_shape=(shape((2, count, gates), BF16), shape((8, waves), F32)),
        in_specs=[hbm] * 7,
        out_specs=(vmem, vmem),
        scratch_shapes=[pltpu.VMEM(a.shape, a.dtype) for a in inputs] + [pltpu.VMEM((count, 8), F32), pltpu.SemaphoreType.DMA((7,))],
        compiler_params=PARAMS,
        name="migrate",
    )(*(pltpu.with_memory_space_constraint(a, pltpu.HBM) for a in inputs))
    blocks = [swap(migrated, by, odd) for by, odd in SLOTS]
    target = swap(params, *DIAGONAL)
    mate = swap(migrated, 1, 0)
    other = swap(params, 1, 0)
    lend_weights = pl.pallas_call(
        lend_weights_kernel,
        out_shape=shape((2, waves, 2 * count), BF16),
        in_specs=[vmem],
        out_specs=vmem,
        scratch_shapes=[pltpu.VMEM((6, waves, 128), F32)],
        compiler_params=PARAMS,
        name="lend_weights",
    )(target)
    lending, lending_ends = pl.pallas_call(
        lend_kernel,
        out_shape=(shape((2, waves, gates), BF16), shape((2, 2 * LOOK, gates), BF16)),
        in_specs=[vmem] * 3,
        out_specs=(vmem, vmem),
        compiler_params=PARAMS,
        name="lend",
    )(lend_weights, migrated, mate)
    lent_ends = swap(lending_ends, *DIAGONAL)
    lent = swap(lending, *DIAGONAL)
    weigh_call = lambda: pl.pallas_call(
        weights_kernel,
        out_shape=(shape((2, waves, gates), F32), shape((2, waves, len(SLOTS) * count), BF16)),
        in_specs=[vmem] * 2,
        out_specs=(vmem, vmem),
        scratch_shapes=[pltpu.VMEM((6, waves, 128), F32), pltpu.VMEM((2, waves, count), BF16)],
        compiler_params=PARAMS,
    )
    partial, weights = weigh_call()(params, migrated)
    partial2, weights2 = weigh_call()(other, migrated)
    focus_call = lambda dtype: pl.pallas_call(
        focus_kernel,
        out_shape=shape((2, waves, gates), dtype),
        in_specs=[vmem] * (2 + len(blocks)),
        out_specs=vmem,
        compiler_params=PARAMS,
    )
    message = focus_call(BF16)(partial2, weights2, *blocks)
    keep = focus_call(F32)(partial, weights, *blocks)
    got = swap(message, 1, 0)
    near, far = pl.pallas_call(
        functools.partial(ends_kernel, devices),
        out_shape=(shape((LOOK, gates), F32),) * 2,
        in_specs=[vmem] * 3,
        out_specs=(vmem, vmem),
        compiler_params=PARAMS,
        name="ends",
    )(keep, got, lent_ends)
    far = beside(far)
    near = swap(near, 1, 0)
    focused, looked, ends = pl.pallas_call(
        functools.partial(power_kernel, devices),
        out_shape=(shape((2, waves, gates), BF16), shape((waves, gates), F32), shape((2 * LOOK, gates), F32)),
        in_specs=[vmem] * 3,
        out_specs=(vmem, vmem, vmem),
        scratch_shapes=[pltpu.VMEM((waves + 2 * LOOK, gates), F32)],
        compiler_params=PARAMS,
        name="power",
    )(keep, got, lent)
    multilook = pl.pallas_call(
        functools.partial(edge_kernel, devices),
        out_shape=shape((waves, gates), F32),
        in_specs=[hbm, vmem, vmem, vmem],
        out_specs=hbm,
        scratch_shapes=[pltpu.VMEM((2, LOOK, gates), F32), pltpu.SemaphoreType.DMA((2,))],
        input_output_aliases={0: 0},
        compiler_params=PARAMS,
        name="edge",
    )(looked, ends, near, far)
    return (focused, multilook)


def solution(mesh):
    part = P(("arcs", "seg"))
    return jax.shard_map(
        shards,
        mesh=mesh,
        in_specs=(P(None, ("arcs", "seg"), None),) + (part,) * 6,
        out_specs=(P(None, ("arcs", "seg"), None), P(("arcs", "seg"), None)),
        check_vma=False,
    )
```

```python
import functools
import math

import jax
import jax.numpy as jnp
from jax import lax
from jax.experimental import pallas as pl
from jax.experimental.pallas import tpu as pltpu
from jax.sharding import PartitionSpec as P


REACH = 4
LOOK = 8
F32 = jnp.float32
BF16 = jnp.bfloat16

SIN = (3.1415927410125732, -5.167710304260254, 2.550077438354492, -0.5982902646064758, 0.07765503972768784)
COS = (0.9999999403953552, -4.934792995452881, 4.058411121368408, -1.3318735361099243, 0.21968165040016174)
SLOTS = ((2, 0), (4, 0), (4, 1))
DIAGONAL = (2, 1)
PARAMS = pltpu.CompilerParams(vmem_limit_bytes=16 * 2**20)


def neighbour(i, by, odd, devices):
    up = (i // by) % 2 == (1 if odd else 0)
    j = i + by if up else i - by
    return j if 0 <= j < devices else i ^ 1


def swap(array, by, odd):
    devices = lax.axis_size("seg")
    return lax.ppermute(array, "seg", [(i, neighbour(i, by, odd, devices)) for i in range(devices)])


def beside(array):
    arcs, devices = lax.axis_size("arcs"), lax.axis_size("seg")
    pairs = []
    for arc in range(arcs):
        for i in range(devices):
            j = i + 1 if i % 2 else i - 1
            to = (arc, j) if 0 <= j < devices else (arc ^ 1, i) if arcs % 2 == 0 else (arc, j % devices)
            pairs.append((arc * devices + i, to[0] * devices + to[1]))
    return lax.ppermute(array, ("arcs", "seg"), pairs)


def migrate_kernel(*refs):
    inputs, (out_ref, params_ref), held, (turned, sems) = refs[:7], refs[7:9], refs[9:16], refs[16:]
    copies = [pltpu.make_async_copy(src, dst, sems.at[k]) for k, (src, dst) in enumerate(zip(inputs, held))]
    for copy in copies:
        copy.start()
    for copy in copies[1:]:
        copy.wait()
    pulses_ref, fraction_ref, shift_ref, start_ref, end_ref, doppler_ref, chirp_ref = held
    _, count, gates = pulses_ref.shape
    params_ref[0:1, :] = start_ref[...].astype(F32)
    params_ref[1:2, :] = end_ref[...].astype(F32)
    params_ref[2:3, :] = doppler_ref[...]
    params_ref[3:4, :] = chirp_ref[...]
    params_ref[4:8, :] = jnp.zeros((4, params_ref.shape[1]), F32)
    spare = jnp.zeros((6, count), F32)
    turned[...] = jnp.transpose(jnp.concatenate([fraction_ref[...], shift_ref[...].astype(F32), spare], 0))
    rows = 64
    lane = lax.broadcasted_iota(jnp.int32, (rows, 128), 1)
    pick = functools.partial(jnp.take_along_axis, axis=1, mode="promise_in_bounds")
    plans = []
    for r in range(0, count, rows):
        fraction = jnp.broadcast_to(turned[r : r + rows, 0:1], (rows, 128))
        shift = jnp.broadcast_to(turned[r : r + rows, 1:2], (rows, 128)).astype(jnp.int32)
        plans.append((r, [(lane + shift, 1.0 - fraction), (lane + shift + 1, fraction)]))
    copies[0].wait()
    for r, terms in plans:
        for part in range(2):
            tiles = [pulses_ref[part, r : r + rows, at : at + 128].astype(F32) for at in range(0, gates, 128)]
            total = [0.0] * len(tiles)
            for at, scale in terms:
                moved = [pick(t, at & 127) for t in tiles] + [0.0]
                for j in range(len(tiles)):
                    total[j] += scale * jnp.where(at < 128, moved[j], moved[j + 1])
            for j, value in enumerate(total):
                out_ref[part, r : r + rows, j * 128 : (j + 1) * 128] = value.astype(BF16)


def poly(coefs, z):
    total = coefs[-1] * z + coefs[-2]
    for c in coefs[-3::-1]:
        total = total * z + c
    return total


def spread(ref, reach, cols):
    waves = ref.shape[1]
    start, end = ref[0:1, :], ref[1:2, :]
    center = jnp.floor((start + end) * 0.5)
    linear = ref[2:3, :] * (1.0 / (math.pi * reach))
    square = ref[3:4, :] * (1.0 / (math.pi * reach * reach))
    scale = lax.rsqrt(end - start)
    turned = jnp.transpose(jnp.concatenate([center, start, end, linear, square, scale, scale, scale], 0))
    for k in range(6):
        cols[k] = jnp.broadcast_to(turned[:, k : k + 1], (waves, 128))


def weigh(cols, base, pulse_count, put, rows=16, unroll=8):
    lanes = range(0, pulse_count, 128)
    at = lax.broadcasted_iota(jnp.int32, (rows, 128), 1) + base
    pulses = [(at + lane).astype(F32) for lane in lanes]

    def step(k, carry):
        r = pl.multiple_of(k * rows, rows)
        center, start, end, linear, square, scale = (cols[j, pl.ds(r, rows), :] for j in range(6))
        minus = -scale
        for lane, pulse in zip(lanes, pulses):
            u = pulse - center
            halves = (square * u + linear) * u
            near = jnp.round(halves)
            rest = halves - near
            z = rest * rest
            signed = jnp.where((near.astype(jnp.int32) & 1) != 0, minus, scale)
            signed = jnp.where((pulse >= start) & (pulse < end), signed, 0.0)
            put(r, lane, signed * poly(COS, z), signed * rest * poly(SIN, z))
        return carry

    lax.fori_loop(0, cols.shape[1] // rows, step, 0, unroll=unroll)


def partner(device, by, odd):
    return jnp.where((device // by) % 2 == odd, device + by, device - by)


dot = functools.partial(jnp.dot, preferred_element_type=F32)


def into(ref, at):
    def put(r, lane, re, im):
        ref[0, pl.ds(r, 16), at + lane : at + lane + 128] = re.astype(BF16)
        ref[1, pl.ds(r, 16), at + lane : at + lane + 128] = im.astype(BF16)

    return put


def lend_weights_kernel(target_ref, out_ref, cols):
    device = lax.axis_index("seg")
    count = out_ref.shape[2] // 2
    mate = device + 1 - 2 * (device % 2)
    spread(target_ref, REACH * count, cols)
    weigh(cols, device * count, count, into(out_ref, 0))
    weigh(cols, mate * count, count, into(out_ref, count))


def lend_kernel(w_ref, own_ref, mate_ref, out_ref, ends_ref):
    count = own_ref.shape[1]
    waves = out_ref.shape[1]
    re, im = w_ref[0], w_ref[1]
    a = dot(re[:, :count], own_ref[0]) + dot(re[:, count:], mate_ref[0])
    b = dot(im[:, :count], own_ref[1]) + dot(im[:, count:], mate_ref[1])
    c = dot(re[:, :count], own_ref[1]) + dot(re[:, count:], mate_ref[1])
    d = dot(im[:, :count], own_ref[0]) + dot(im[:, count:], mate_ref[0])
    for part, value in enumerate((a - b, c + d)):
        out_ref[part] = value.astype(BF16)
        ends_ref[part] = jnp.concatenate([value[:LOOK], value[waves - LOOK :]], 0).astype(BF16)


def weights_kernel(params_ref, own_ref, partial_ref, weights_ref, cols, own_w):
    device = lax.axis_index("seg")
    count = own_ref.shape[1]
    spread(params_ref, REACH * count, cols)
    weigh(cols, device * count, count, into(own_w, 0))
    partial_ref[0] = dot(own_w[0], own_ref[0]) - dot(own_w[1], own_ref[1])
    partial_ref[1] = dot(own_w[0], own_ref[1]) + dot(own_w[1], own_ref[0])
    for slot, (by, odd) in enumerate(SLOTS):
        weigh(cols, partner(device, by, odd) * count, count, into(weights_ref, slot * count))


def focus_kernel(partial_ref, weights_ref, *refs):
    blocks, out_ref = refs[:-1], refs[-1]
    count = blocks[0].shape[1]
    re, im = partial_ref[0], partial_ref[1]
    minus = jnp.zeros_like(re)
    for slot, ref in enumerate(blocks):
        w_re = weights_ref[0, :, slot * count : (slot + 1) * count]
        w_im = weights_ref[1, :, slot * count : (slot + 1) * count]
        re += dot(w_re, ref[0])
        minus += dot(w_im, ref[1])
        im += dot(w_re, ref[1])
        im += dot(w_im, ref[0])
    out_ref[0] = (re - minus).astype(out_ref.dtype)
    out_ref[1] = im.astype(out_ref.dtype)


def total_of(devices, keep, got, lent):
    by_chip = partner(lax.axis_index("seg"), *DIAGONAL)
    known = (by_chip >= 0) & (by_chip < devices)
    return keep + got.astype(F32) + jnp.where(known, lent.astype(F32), 0.0)


def ends_kernel(devices, keep_ref, got_ref, lent_ref, near_ref, far_ref):
    waves = keep_ref.shape[1]
    pair = slice(0, 2 * LOOK), slice(waves - 2 * LOOK, waves)
    keep, got = (
        jnp.concatenate([ref[:, pair[0]].astype(F32)[:, :LOOK], ref[:, pair[1]].astype(F32)[:, LOOK:]], 1)
        for ref in (keep_ref, got_ref)
    )
    total = total_of(devices, keep, got, lent_ref[...])
    power = total[0] * total[0] + total[1] * total[1]
    initial, last = power[:LOOK], power[LOOK:]
    core = lax.axis_index("seg") % 2
    near_ref[...] = jnp.where(core == 0, last, initial)
    far_ref[...] = jnp.where(core == 0, initial, last)


def power_kernel(devices, keep_ref, got_ref, lent_ref, focused_ref, looked_ref, ends_ref, ext):
    waves = focused_ref.shape[1]
    total = total_of(devices, keep_ref[...], got_ref[...], lent_ref[...])
    focused_ref[...] = total.astype(BF16)
    ext[:LOOK] = jnp.zeros((LOOK, ext.shape[1]), F32)
    ext[LOOK : LOOK + waves] = total[0] * total[0] + total[1] * total[1]
    ext[LOOK + waves :] = jnp.zeros((LOOK, ext.shape[1]), F32)
    rows = waves + 2 * LOOK
    span, window = 1, ext[...]
    while span < 2 * LOOK:
        rows -= span
        window = window[:rows] + window[span : span + rows]
        span *= 2
    looked = (window[:waves] + ext[2 * LOOK :]) * (1.0 / (2 * LOOK + 1))
    looked_ref[...] = looked
    ends_ref[:LOOK] = looked[:LOOK]
    ends_ref[LOOK:] = looked[waves - LOOK :]


def edge_kernel(devices, looked_ref, ends_ref, near_ref, far_ref, out_ref, rows, sems):
    device = lax.axis_index("seg")
    core = device % 2
    beside = device + 2 * core - 1
    scale = 1.0 / (2 * LOOK + 1)
    near = near_ref[...] * scale
    far = far_ref[...] * jnp.where((beside >= 0) & (beside < devices), scale, 0.0)
    row = lax.broadcasted_iota(jnp.int32, near.shape, 0)
    before, after = jnp.where(core == 0, far, near), jnp.where(core == 0, near, far)
    top, bottom = ends_ref[:LOOK], ends_ref[LOOK:]
    for h in range(LOOK):
        top += jnp.where(row <= h, before[h : h + 1, :], 0.0)
        bottom += jnp.where(row >= h, after[h : h + 1, :], 0.0)
    rows[0] = top
    rows[1] = bottom
    waves = out_ref.shape[0]
    copies = [
        pltpu.make_async_copy(rows.at[k], out_ref.at[pl.ds(at, LOOK)], sems.at[k])
        for k, at in enumerate((0, waves - LOOK))
    ]
    for copy in copies:
        copy.start()
    for copy in copies:
        copy.wait()


def shards(pulses, fraction, gate_shift, aperture_start, aperture_end, doppler, chirp_rate):
    _, count, gates = pulses.shape
    waves = aperture_start.shape[0]
    devices = lax.axis_size("seg")
    shape = jax.ShapeDtypeStruct
    vmem = pl.BlockSpec(memory_space=pltpu.VMEM)
    hbm = pl.BlockSpec(memory_space=pltpu.HBM)

    inputs = (
        pulses,
        fraction.reshape(1, count),
        gate_shift.reshape(1, count),
        aperture_start.reshape(1, waves),
        aperture_end.reshape(1, waves),
        doppler.reshape(1, waves),
        chirp_rate.reshape(1, waves),
    )
    migrated, params = pl.pallas_call(
        migrate_kernel,
        out_shape=(shape((2, count, gates), BF16), shape((8, waves), F32)),
        in_specs=[hbm] * 7,
        out_specs=(vmem, vmem),
        scratch_shapes=[pltpu.VMEM(a.shape, a.dtype) for a in inputs] + [pltpu.VMEM((count, 8), F32), pltpu.SemaphoreType.DMA((7,))],
        compiler_params=PARAMS,
        name="migrate",
    )(*(pltpu.with_memory_space_constraint(a, pltpu.HBM) for a in inputs))
    blocks = [swap(migrated, by, odd) for by, odd in SLOTS]
    target = swap(params, *DIAGONAL)
    mate = swap(migrated, 1, 0)
    other = swap(params, 1, 0)
    lend_weights = pl.pallas_call(
        lend_weights_kernel,
        out_shape=shape((2, waves, 2 * count), BF16),
        in_specs=[vmem],
        out_specs=vmem,
        scratch_shapes=[pltpu.VMEM((6, waves, 128), F32)],
        compiler_params=PARAMS,
        name="lend_weights",
    )(target)
    lending, lending_ends = pl.pallas_call(
        lend_kernel,
        out_shape=(shape((2, waves, gates), BF16), shape((2, 2 * LOOK, gates), BF16)),
        in_specs=[vmem] * 3,
        out_specs=(vmem, vmem),
        compiler_params=PARAMS,
        name="lend",
    )(lend_weights, migrated, mate)
    lent_ends = swap(lending_ends, *DIAGONAL)
    lent = swap(lending, *DIAGONAL)
    weigh_call = lambda: pl.pallas_call(
        weights_kernel,
        out_shape=(shape((2, waves, gates), F32), shape((2, waves, len(SLOTS) * count), BF16)),
        in_specs=[vmem] * 2,
        out_specs=(vmem, vmem),
        scratch_shapes=[pltpu.VMEM((6, waves, 128), F32), pltpu.VMEM((2, waves, count), BF16)],
        compiler_params=PARAMS,
    )
    partial, weights = weigh_call()(params, migrated)
    partial2, weights2 = weigh_call()(other, migrated)
    focus_call = lambda dtype: pl.pallas_call(
        focus_kernel,
        out_shape=shape((2, waves, gates), dtype),
        in_specs=[vmem] * (2 + len(blocks)),
        out_specs=vmem,
        compiler_params=PARAMS,
    )
    message = focus_call(BF16)(partial2, weights2, *blocks)
    keep = focus_call(F32)(partial, weights, *blocks)
    got = swap(message, 1, 0)
    near, far = pl.pallas_call(
        functools.partial(ends_kernel, devices),
        out_shape=(shape((LOOK, gates), F32),) * 2,
        in_specs=[vmem] * 3,
        out_specs=(vmem, vmem),
        compiler_params=PARAMS,
        name="ends",
    )(keep, got, lent_ends)
    far = beside(far)
    near = swap(near, 1, 0)
    focused, looked, ends = pl.pallas_call(
        functools.partial(power_kernel, devices),
        out_shape=(shape((2, waves, gates), BF16), shape((waves, gates), F32), shape((2 * LOOK, gates), F32)),
        in_specs=[vmem] * 3,
        out_specs=(vmem, vmem, vmem),
        scratch_shapes=[pltpu.VMEM((waves + 2 * LOOK, gates), F32)],
        compiler_params=PARAMS,
        name="power",
    )(keep, got, lent)
    multilook = pl.pallas_call(
        functools.partial(edge_kernel, devices),
        out_shape=shape((waves, gates), F32),
        in_specs=[hbm, vmem, vmem, vmem],
        out_specs=hbm,
        scratch_shapes=[pltpu.VMEM((2, LOOK, gates), F32), pltpu.SemaphoreType.DMA((2,))],
        input_output_aliases={0: 0},
        compiler_params=PARAMS,
        name="edge",
    )(looked, ends, near, far)
    return (focused, multilook)


def solution(mesh):
    part = P(("arcs", "seg"))
    return jax.shard_map(
        shards,
        mesh=mesh,
        in_specs=(P(None, ("arcs", "seg"), None),) + (part,) * 6,
        out_specs=(P(None, ("arcs", "seg"), None), P(("arcs", "seg"), None)),
        check_vma=False,
    )
```

```python
import functools
import math

import jax
import jax.numpy as jnp
from jax import lax
from jax.experimental import pallas as pl
from jax.experimental.pallas import tpu as pltpu
from jax.sharding import PartitionSpec as P


REACH = 4
LOOK = 8
F32 = jnp.float32
BF16 = jnp.bfloat16

SIN = (3.1415927410125732, -5.167710304260254, 2.550077438354492, -0.5982902646064758, 0.07765503972768784)
COS = (0.9999999403953552, -4.934792995452881, 4.058411121368408, -1.3318735361099243, 0.21968165040016174)
SLOTS = ((2, 0), (4, 0), (4, 1))
DIAGONAL = (2, 1)
PARAMS = pltpu.CompilerParams(vmem_limit_bytes=16 * 2**20)


def neighbour(i, by, odd, devices):
    up = (i // by) % 2 == (1 if odd else 0)
    j = i + by if up else i - by
    return j if 0 <= j < devices else i ^ 1


def swap(array, by, odd):
    devices = lax.axis_size("seg")
    return lax.ppermute(array, "seg", [(i, neighbour(i, by, odd, devices)) for i in range(devices)])


def beside(array):
    arcs, devices = lax.axis_size("arcs"), lax.axis_size("seg")
    pairs = []
    for arc in range(arcs):
        for i in range(devices):
            j = i + 1 if i % 2 else i - 1
            to = (arc, j) if 0 <= j < devices else (arc ^ 1, i) if arcs % 2 == 0 else (arc, j % devices)
            pairs.append((arc * devices + i, to[0] * devices + to[1]))
    return lax.ppermute(array, ("arcs", "seg"), pairs)


def gather_kernel(*refs):
    inputs, pulses_in, (params_ref, turned_ref, pulses_ref), held, sems = refs[:6], refs[6], refs[7:10], refs[10:16], refs[16]
    whole = pltpu.make_async_copy(pulses_in, pulses_ref, sems.at[6])
    whole.start()
    copies = [pltpu.make_async_copy(src, dst, sems.at[k]) for k, (src, dst) in enumerate(zip(inputs, held))]
    for copy in copies:
        copy.start()
    for copy in copies:
        copy.wait()
    fraction_ref, shift_ref, start_ref, end_ref, doppler_ref, chirp_ref = held
    params_ref[0:1, :] = start_ref[...].astype(F32)
    params_ref[1:2, :] = end_ref[...].astype(F32)
    params_ref[2:3, :] = doppler_ref[...]
    params_ref[3:4, :] = chirp_ref[...]
    params_ref[4:8, :] = jnp.zeros((4, params_ref.shape[1]), F32)
    spare = jnp.zeros((6, fraction_ref.shape[1]), F32)
    turned_ref[...] = jnp.transpose(jnp.concatenate([fraction_ref[...], shift_ref[...].astype(F32), spare], 0))
    whole.wait()


def migrate_kernel(pulses_ref, turned, out_ref):
    _, count, gates = pulses_ref.shape
    rows = 64
    lane = lax.broadcasted_iota(jnp.int32, (rows, 128), 1)
    pick = functools.partial(jnp.take_along_axis, axis=1, mode="promise_in_bounds")
    plans = []
    for r in range(0, count, rows):
        fraction = jnp.broadcast_to(turned[r : r + rows, 0:1], (rows, 128))
        shift = jnp.broadcast_to(turned[r : r + rows, 1:2], (rows, 128)).astype(jnp.int32)
        plans.append((r, [(lane + shift, 1.0 - fraction), (lane + shift + 1, fraction)]))
    for r, terms in plans:
        for part in range(2):
            tiles = [pulses_ref[part, r : r + rows, at : at + 128].astype(F32) for at in range(0, gates, 128)]
            total = [0.0] * len(tiles)
            for at, scale in terms:
                moved = [pick(t, at & 127) for t in tiles] + [0.0]
                for j in range(len(tiles)):
                    total[j] += scale * jnp.where(at < 128, moved[j], moved[j + 1])
            for j, value in enumerate(total):
                out_ref[part, r : r + rows, j * 128 : (j + 1) * 128] = value.astype(BF16)


def poly(coefs, z):
    total = coefs[-1] * z + coefs[-2]
    for c in coefs[-3::-1]:
        total = total * z + c
    return total


def spread(ref, reach, cols):
    waves = ref.shape[1]
    start, end = ref[0:1, :], ref[1:2, :]
    center = jnp.floor((start + end) * 0.5)
    linear = ref[2:3, :] * (1.0 / (math.pi * reach))
    square = ref[3:4, :] * (1.0 / (math.pi * reach * reach))
    scale = lax.rsqrt(end - start)
    turned = jnp.transpose(jnp.concatenate([center, start, end, linear, square, scale, scale, scale], 0))
    for k in range(6):
        cols[k] = jnp.broadcast_to(turned[:, k : k + 1], (waves, 128))


def weigh(cols, base, pulse_count, put, rows=16, unroll=8):
    lanes = range(0, pulse_count, 128)
    at = lax.broadcasted_iota(jnp.int32, (rows, 128), 1) + base
    pulses = [(at + lane).astype(F32) for lane in lanes]

    def step(k, carry):
        r = pl.multiple_of(k * rows, rows)
        center, start, end, linear, square, scale = (cols[j, pl.ds(r, rows), :] for j in range(6))
        minus = -scale
        for lane, pulse in zip(lanes, pulses):
            u = pulse - center
            halves = (square * u + linear) * u
            near = jnp.round(halves)
            rest = halves - near
            z = rest * rest
            signed = jnp.where((near.astype(jnp.int32) & 1) != 0, minus, scale)
            signed = jnp.where((pulse >= start) & (pulse < end), signed, 0.0)
            put(r, lane, signed * poly(COS, z), signed * rest * poly(SIN, z))
        return carry

    lax.fori_loop(0, cols.shape[1] // rows, step, 0, unroll=unroll)


def partner(device, by, odd):
    return jnp.where((device // by) % 2 == odd, device + by, device - by)


dot = functools.partial(jnp.dot, preferred_element_type=F32)


def into(ref, at):
    def put(r, lane, re, im):
        ref[0, pl.ds(r, 16), at + lane : at + lane + 128] = re.astype(BF16)
        ref[1, pl.ds(r, 16), at + lane : at + lane + 128] = im.astype(BF16)

    return put


def lend_weights_kernel(target_ref, out_ref, cols):
    device = lax.axis_index("seg")
    count = out_ref.shape[2] // 2
    mate = device + 1 - 2 * (device % 2)
    spread(target_ref, REACH * count, cols)
    weigh(cols, device * count, count, into(out_ref, 0))
    weigh(cols, mate * count, count, into(out_ref, count))


def lend_kernel(w_ref, own_ref, mate_ref, out_ref, ends_ref):
    count = own_ref.shape[1]
    waves = out_ref.shape[1]
    re, im = w_ref[0], w_ref[1]
    a = dot(re[:, :count], own_ref[0]) + dot(re[:, count:], mate_ref[0])
    b = dot(im[:, :count], own_ref[1]) + dot(im[:, count:], mate_ref[1])
    c = dot(re[:, :count], own_ref[1]) + dot(re[:, count:], mate_ref[1])
    d = dot(im[:, :count], own_ref[0]) + dot(im[:, count:], mate_ref[0])
    for part, value in enumerate((a - b, c + d)):
        out_ref[part] = value.astype(BF16)
        ends_ref[part] = jnp.concatenate([value[:LOOK], value[waves - LOOK :]], 0).astype(BF16)


def own_kernel(params_ref, own_ref, partial_ref, cols, own_w):
    count = own_ref.shape[1]
    spread(params_ref, REACH * count, cols)
    weigh(cols, lax.axis_index("seg") * count, count, into(own_w, 0))
    partial_ref[0] = dot(own_w[0], own_ref[0]) - dot(own_w[1], own_ref[1])
    partial_ref[1] = dot(own_w[0], own_ref[1]) + dot(own_w[1], own_ref[0])


def weights_kernel(cols, weights_ref):
    device = lax.axis_index("seg")
    count = weights_ref.shape[2] // len(SLOTS)
    for slot, (by, odd) in enumerate(SLOTS):
        weigh(cols, partner(device, by, odd) * count, count, into(weights_ref, slot * count))


def focus_kernel(partial_ref, weights_ref, *refs):
    blocks, (out_ref, ends_ref) = refs[:-2], refs[-2:]
    count = blocks[0].shape[1]
    waves = out_ref.shape[1]
    re, im = partial_ref[0], partial_ref[1]
    minus = jnp.zeros_like(re)
    for slot, ref in enumerate(blocks):
        w_re = weights_ref[0, :, slot * count : (slot + 1) * count]
        w_im = weights_ref[1, :, slot * count : (slot + 1) * count]
        re += dot(w_re, ref[0])
        minus += dot(w_im, ref[1])
        im += dot(w_re, ref[1])
        im += dot(w_im, ref[0])
    for part, value in enumerate((re - minus, im)):
        out_ref[part] = value.astype(out_ref.dtype)
        ends_ref[part] = jnp.concatenate([value[:LOOK], value[waves - LOOK :]], 0).astype(out_ref.dtype)


def total_of(devices, keep, got, lent):
    by_chip = partner(lax.axis_index("seg"), *DIAGONAL)
    known = (by_chip >= 0) & (by_chip < devices)
    return keep + got.astype(F32) + jnp.where(known, lent.astype(F32), 0.0)


def ends_kernel(devices, keep_ref, got_ref, lent_ref, near_ref, far_ref):
    total = total_of(devices, keep_ref[...], got_ref[...], lent_ref[...])
    power = total[0] * total[0] + total[1] * total[1]
    initial, last = power[:LOOK], power[LOOK:]
    core = lax.axis_index("seg") % 2
    near_ref[...] = jnp.where(core == 0, last, initial)
    far_ref[...] = jnp.where(core == 0, initial, last)


def power_kernel(devices, keep_ref, got_ref, lent_ref, focused_ref, looked_ref, ends_ref, ext):
    waves = focused_ref.shape[1]
    total = total_of(devices, keep_ref[...], got_ref[...], lent_ref[...])
    focused_ref[...] = total.astype(BF16)
    ext[:LOOK] = jnp.zeros((LOOK, ext.shape[1]), F32)
    ext[LOOK : LOOK + waves] = total[0] * total[0] + total[1] * total[1]
    ext[LOOK + waves :] = jnp.zeros((LOOK, ext.shape[1]), F32)
    rows = waves + 2 * LOOK
    span, window = 1, ext[...]
    while span < 2 * LOOK:
        rows -= span
        window = window[:rows] + window[span : span + rows]
        span *= 2
    looked = (window[:waves] + ext[2 * LOOK :]) * (1.0 / (2 * LOOK + 1))
    looked_ref[...] = looked
    ends_ref[:LOOK] = looked[:LOOK]
    ends_ref[LOOK:] = looked[waves - LOOK :]


def edge_kernel(devices, looked_ref, ends_ref, near_ref, far_ref, out_ref, rows, sems):
    device = lax.axis_index("seg")
    core = device % 2
    beside = device + 2 * core - 1
    scale = 1.0 / (2 * LOOK + 1)
    near = near_ref[...] * scale
    far = far_ref[...] * jnp.where((beside >= 0) & (beside < devices), scale, 0.0)
    row = lax.broadcasted_iota(jnp.int32, near.shape, 0)
    before, after = jnp.where(core == 0, far, near), jnp.where(core == 0, near, far)
    top, bottom = ends_ref[:LOOK], ends_ref[LOOK:]
    for h in range(LOOK):
        top += jnp.where(row <= h, before[h : h + 1, :], 0.0)
        bottom += jnp.where(row >= h, after[h : h + 1, :], 0.0)
    rows[0] = top
    rows[1] = bottom
    waves = out_ref.shape[0]
    copies = [
        pltpu.make_async_copy(rows.at[k], out_ref.at[pl.ds(at, LOOK)], sems.at[k])
        for k, at in enumerate((0, waves - LOOK))
    ]
    for copy in copies:
        copy.start()
    for copy in copies:
        copy.wait()


def shards(pulses, fraction, gate_shift, aperture_start, aperture_end, doppler, chirp_rate):
    _, count, gates = pulses.shape
    waves = aperture_start.shape[0]
    devices = lax.axis_size("seg")
    shape = jax.ShapeDtypeStruct
    vmem = pl.BlockSpec(memory_space=pltpu.VMEM)
    hbm = pl.BlockSpec(memory_space=pltpu.HBM)

    inputs = (
        fraction.reshape(1, count),
        gate_shift.reshape(1, count),
        aperture_start.reshape(1, waves),
        aperture_end.reshape(1, waves),
        doppler.reshape(1, waves),
        chirp_rate.reshape(1, waves),
    )
    params, turned, held_pulses = pl.pallas_call(
        gather_kernel,
        out_shape=(shape((8, waves), F32), shape((count, 8), F32), shape(pulses.shape, pulses.dtype)),
        in_specs=[hbm] * 7,
        out_specs=(vmem, vmem, vmem),
        scratch_shapes=[pltpu.VMEM(a.shape, a.dtype) for a in inputs] + [pltpu.SemaphoreType.DMA((7,))],
        compiler_params=PARAMS,
        name="gather",
    )(*(pltpu.with_memory_space_constraint(a, pltpu.HBM) for a in inputs + (pulses,)))
    migrated = pl.pallas_call(
        migrate_kernel,
        out_shape=shape((2, count, gates), BF16),
        in_specs=[vmem] * 2,
        out_specs=vmem,
        compiler_params=PARAMS,
        name="migrate",
    )(held_pulses, turned)
    blocks = [swap(migrated, by, odd) for by, odd in SLOTS]
    target = swap(params, *DIAGONAL)
    mate = swap(migrated, 1, 0)
    other = swap(params, 1, 0)
    lend_weights = pl.pallas_call(
        lend_weights_kernel,
        out_shape=shape((2, waves, 2 * count), BF16),
        in_specs=[vmem],
        out_specs=vmem,
        scratch_shapes=[pltpu.VMEM((6, waves, 128), F32)],
        compiler_params=PARAMS,
        name="lend_weights",
    )(target)
    lending, lending_ends = pl.pallas_call(
        lend_kernel,
        out_shape=(shape((2, waves, gates), BF16), shape((2, 2 * LOOK, gates), BF16)),
        in_specs=[vmem] * 3,
        out_specs=(vmem, vmem),
        compiler_params=PARAMS,
        name="lend",
    )(lend_weights, migrated, mate)
    lent_ends = swap(lending_ends, *DIAGONAL)
    lent = swap(lending, *DIAGONAL)
    own_call = lambda: pl.pallas_call(
        own_kernel,
        out_shape=(shape((2, waves, gates), F32), shape((6, waves, 128), F32)),
        in_specs=[vmem] * 2,
        out_specs=(vmem, vmem),
        scratch_shapes=[pltpu.VMEM((2, waves, count), BF16)],
        compiler_params=PARAMS,
    )
    weigh_call = lambda: pl.pallas_call(
        weights_kernel,
        out_shape=shape((2, waves, len(SLOTS) * count), BF16),
        in_specs=[vmem],
        out_specs=vmem,
        compiler_params=PARAMS,
    )
    focus_call = lambda dtype: pl.pallas_call(
        focus_kernel,
        out_shape=(shape((2, waves, gates), dtype), shape((2, 2 * LOOK, gates), dtype)),
        in_specs=[vmem] * (2 + len(blocks)),
        out_specs=(vmem, vmem),
        compiler_params=PARAMS,
    )
    partial, cols = own_call()(params, migrated)
    partial2, cols2 = own_call()(other, migrated)
    message, message_ends = focus_call(BF16)(partial2, weigh_call()(cols2), *blocks)
    keep, keep_ends = focus_call(F32)(partial, weigh_call()(cols), *blocks)
    got_ends = swap(message_ends, 1, 0)
    got = swap(message, 1, 0)
    near, far = pl.pallas_call(
        functools.partial(ends_kernel, devices),
        out_shape=(shape((LOOK, gates), F32),) * 2,
        in_specs=[vmem] * 3,
        out_specs=(vmem, vmem),
        compiler_params=PARAMS,
        name="ends",
    )(keep_ends, got_ends, lent_ends)
    far = beside(far)
    near = swap(near, 1, 0)
    focused, looked, ends = pl.pallas_call(
        functools.partial(power_kernel, devices),
        out_shape=(shape((2, waves, gates), BF16), shape((waves, gates), F32), shape((2 * LOOK, gates), F32)),
        in_specs=[vmem] * 3,
        out_specs=(vmem, vmem, vmem),
        scratch_shapes=[pltpu.VMEM((waves + 2 * LOOK, gates), F32)],
        compiler_params=PARAMS,
        name="power",
    )(keep, got, lent)
    multilook = pl.pallas_call(
        functools.partial(edge_kernel, devices),
        out_shape=shape((waves, gates), F32),
        in_specs=[hbm, vmem, vmem, vmem],
        out_specs=hbm,
        scratch_shapes=[pltpu.VMEM((2, LOOK, gates), F32), pltpu.SemaphoreType.DMA((2,))],
        input_output_aliases={0: 0},
        compiler_params=PARAMS,
        name="edge",
    )(looked, ends, near, far)
    return (focused, multilook)


def solution(mesh):
    part = P(("arcs", "seg"))
    return jax.shard_map(
        shards,
        mesh=mesh,
        in_specs=(P(None, ("arcs", "seg"), None),) + (part,) * 6,
        out_specs=(P(None, ("arcs", "seg"), None), P(("arcs", "seg"), None)),
        check_vma=False,
    )
```
